256 devices in a mesh: seq: 128 (over x, y, z), resp: 2 (over core).
Axes of the slice: x: 4, y: 4, z: 8, core: 2. Of those that a mesh axis runs over, the one named last changes fastest.
Arguments:
- cat_query: bfloat16 [16384, 4096], P('seq', 'resp'), may hold values from -6 to 6
- cat_key: bfloat16 [16384, 4096], P('seq', 'resp'), may hold values from -6 to 6
- cat_value: bfloat16 [16384, 4096], P('seq', 'resp'), may hold values from -6 to 6
- resp_query: bfloat16 [32768, 4096], P(('seq', 'resp')), may hold values from -6 to 6
- resp_key: bfloat16 [32768, 4096], P(('seq', 'resp')), may hold values from -6 to 6
- resp_value: bfloat16 [32768, 4096], P(('seq', 'resp')), may hold values from -6 to 6
- resp_lengths: int32 [256, 3], P(('seq', 'resp')), may hold values from 1 to 64, 128 in all within a row
- norm_gain: float32 [4096], replicated, may hold values from 0.1 to 1.9
Outputs:
- cat_out: bfloat16 [16384, 4096], P('seq', 'resp')
- resp_out: bfloat16 [32768, 4096], P(('seq', 'resp'))
The draws below stay inside these ranges and needn't reach their ends.
Inputs may be any that keep to these rules, and one draw needn't show every extreme that they name: `resp_lengths`: each row's 3 lengths sum to 128.
All inputs are finite; a program needn't handle non-finite values.
Results may differ from the reference program's by a relative error of at most 0.0021.
Values sent between devices are 32-bit elements; how exact they have to be, the bound alone decides.
A program may use at most 320 MiB of HBM per device.

```python
import math
import jax
import jax.numpy as jnp
import numpy as np
from jax import lax

H = 32
DH = 128
CAT_DEV = 128
RESP_DEV = 128
SEGS = 3
D = 4096
CAT = 16384
PACKS = 256
RESP = 32768


def levels(rng, extent, shards, least, largest):
    def one(dim, parts):
        draws = jax.random.uniform(jax.random.fold_in(jax.random.fold_in(rng, 6), dim), (parts,), jnp.float32, least / len(shards), largest / len(shards))
        return jnp.repeat(jnp.exp(draws), extent[dim] // parts).reshape((-1,) + (1,) * (len(extent) - dim - 1))

    factor_of = one(*shards[0])
    for cut in shards[1:]:
        factor_of = factor_of * one(*cut)
    return factor_of


def length_profile(count, total, reach, lean):
    weights = [(1 << 20) // math.isqrt(standing ** lean) + 1 for standing in range(2, count + 1)]
    surplus, holding = total - reach - (count - 1), [1] * (count - 1)
    while surplus > 0:
        free = [i for i in range(count - 1) if holding[i] < reach]
        mass, remaining = sum([weights[i] for i in free]), surplus
        for i in free:
            addition = min(reach - holding[i], max(1, remaining * weights[i] // mass), surplus)
            holding[i] = holding[i] + addition
            surplus = surplus - addition
    return np.array([reach] + holding)


def uneven(key, amount, total, limit, slope):
    if amount == 2:
        one = jax.random.randint(key, (), max(1, total - limit), min(limit, total - 1) + 1)
        return jnp.stack([one, total - one])
    sizes = jnp.asarray(length_profile(amount, total, limit, slope), jnp.int32)
    twos = (amount - 1) // 2
    donor, receiver = sizes[1:1 + 2 * twos:2], sizes[2:2 + 2 * twos:2]
    slack = jnp.minimum(donor - 1, limit - receiver)
    shifted = jax.random.randint(jax.random.fold_in(key, 1), (twos,), 0, 1 << 20) % (slack + 1)
    sizes = sizes.at[1:1 + 2 * twos:2].set(donor - shifted).at[2:2 + 2 * twos:2].set(receiver + shifted)
    return sizes[jax.random.permutation(jax.random.fold_in(key, 2), amount)]


def centred(rng, shape, deviation, limit, cuts=(), held_as=jnp.bfloat16):
    loudness = levels(rng, shape, cuts, -0.22, 0.18) if cuts else 1.0
    result = jax.random.normal(rng, shape, jnp.float32) * deviation * loudness
    return jnp.minimum(jnp.maximum(result, -limit), limit).astype(held_as)


def setup_inputs(seed: int = 0) -> dict:
    streams_of = jax.random.split(jax.random.key(seed), 9)
    return {
        "cat_query": centred(streams_of[0], (CAT, D), 1.0, 6.0, ((0, 128), (1, 2))),
        "cat_key": centred(streams_of[1], (CAT, D), 1.0, 6.0, ((0, 128), (1, 2))),
        "cat_value": centred(streams_of[2], (CAT, D), 1.0, 6.0, ((0, 128), (1, 2))),
        "resp_query": centred(streams_of[3], (RESP, D), 1.0, 6.0, ((0, 256),)),
        "resp_key": centred(streams_of[4], (RESP, D), 1.0, 6.0, ((0, 256),)),
        "resp_value": centred(streams_of[5], (RESP, D), 1.0, 6.0, ((0, 256),)),
        "resp_lengths": jax.vmap(lambda own: uneven(own, SEGS, RESP_DEV, RESP_DEV // 2, 0))(jax.random.split(streams_of[6], PACKS)).reshape((PACKS, SEGS)).astype(jnp.int32),
        "norm_gain": jnp.clip(1.0 + 0.18 * jax.random.normal(streams_of[7], (D,), jnp.float32), 0.1, 1.9),
    }


def attend(query, key, value, mask, state, heads):
    rows = query.shape[0]
    qh = query.reshape(rows, heads, DH).astype(jnp.float32)
    kh = key.reshape(rows, heads, DH).astype(jnp.float32)
    vh = value.reshape(rows, heads, DH).astype(jnp.float32)
    scores = jnp.einsum('thd,shd->hts', qh, kh)
    scores = jnp.where(mask[None, :, :], scores, 0.0).astype(jnp.bfloat16).astype(jnp.float32)
    inner = jnp.einsum('hts,shd->thd', scores, vh)
    outer = jnp.einsum('thd,hde->the', qh, state, precision=lax.Precision.HIGHEST)
    local_state = jnp.einsum('shd,she->hde', kh, vh)
    return (inner + outer, local_state)

def head_norm(raw, gain, heads):
    square = lax.optimization_barrier(jnp.mean(raw * raw, axis=-1, keepdims=True))
    scaled = raw / jnp.sqrt(square + 1e-06) * gain.reshape(heads, DH)
    return scaled.reshape(raw.shape[0], heads * DH).astype(jnp.bfloat16)

def reference(cat_query, cat_key, cat_value, resp_query, resp_key, resp_value, resp_lengths, norm_gain):
    blocks = CAT // CAT_DEV
    places = jnp.arange(CAT_DEV, dtype=jnp.int32)
    causal = places[None, :] <= places[:, None]
    stacked = (cat_query.reshape(blocks, CAT_DEV, H * DH), cat_key.reshape(blocks, CAT_DEV, H * DH), cat_value.reshape(blocks, CAT_DEV, H * DH))

    def advance(state, block):
        raw, local_state = attend(block[0], block[1], block[2], causal, state, H)
        return (state + local_state, head_norm(raw, norm_gain, H))
    start = jnp.zeros((H, DH, DH), jnp.float32)
    final, cat_blocks = lax.scan(advance, start, stacked)
    cat_out = cat_blocks.reshape(CAT, H * DH)
    packs = RESP // RESP_DEV
    rows = jnp.arange(RESP_DEV, dtype=jnp.int32)

    def one_pack(items):
        query, key, value, lengths = items
        ends = jnp.cumsum(lengths).astype(jnp.int32)
        segment = lax.optimization_barrier(jnp.sum((rows[:, None] >= ends[None, :]).astype(jnp.int32), axis=1))
        mask = (segment[:, None] == segment[None, :]) & (rows[None, :] <= rows[:, None])
        raw, unused = attend(query, key, value, mask, final, H)
        return head_norm(raw, norm_gain, H)
    resp_blocks = lax.map(one_pack, (resp_query.reshape(packs, RESP_DEV, H * DH), resp_key.reshape(packs, RESP_DEV, H * DH), resp_value.reshape(packs, RESP_DEV, H * DH), resp_lengths))
    return (cat_out, resp_blocks.reshape(RESP, H * DH))
```

```python
import jax
import jax.numpy as jnp
from jax import lax
from jax.sharding import PartitionSpec as P

DH = 128


def attend_inner(query, key, value, mask, heads):
    rows = query.shape[0]
    qh = query.reshape(rows, heads, DH)
    kh = key.reshape(rows, heads, DH)
    vh = value.reshape(rows, heads, DH)
    scores = jnp.einsum("thd,shd->hts", qh, kh, preferred_element_type=jnp.float32)
    scores = jnp.where(mask[None, :, :], scores, 0.0).astype(jnp.bfloat16)
    return jnp.einsum("hts,shd->thd", scores, vh, preferred_element_type=jnp.float32)


def attend_outer(query, state, heads):
    rows = query.shape[0]
    qh = query.reshape(rows, heads, DH).astype(jnp.float32)
    return jnp.einsum("thd,hde->the", qh, state, precision=lax.Precision.HIGHEST)


def block_state(key, value, heads):
    rows = key.shape[0]
    kh = key.reshape(rows, heads, DH)
    vh = value.reshape(rows, heads, DH)
    return jnp.einsum("shd,she->hde", kh, vh, preferred_element_type=jnp.float32)


def head_norm(raw, gain, heads):
    square = jnp.mean(raw * raw, axis=-1, keepdims=True)
    scaled = raw * lax.rsqrt(square + 1e-06) * gain.reshape(heads, DH)
    return scaled.reshape(raw.shape[0], heads * DH).astype(jnp.bfloat16)


def transpose_scan(local_state):
    peers = lax.axis_size("seq")
    chunks = local_state.reshape(peers, -1, DH)
    gathered = lax.all_to_all(chunks, "seq", 0, 0, tiled=True)
    inclusive = jnp.cumsum(gathered, axis=0)
    exclusive = jnp.concatenate([jnp.zeros_like(inclusive[:1]), inclusive[:-1]], axis=0)
    prefix = lax.all_to_all(exclusive, "seq", 0, 0, tiled=True)
    return prefix.reshape(local_state.shape), inclusive[-1]


def per_device(
    cat_query, cat_key, cat_value, resp_query, resp_key, resp_value, resp_lengths, norm_gain
):
    heads_here = cat_query.shape[1] // DH
    all_heads = resp_query.shape[1] // DH
    local_state = block_state(cat_key, cat_value, heads_here)
    prefix, total_chunk = transpose_scan(local_state)
    whole = lax.all_gather(total_chunk, ("resp", "seq"), axis=0, tiled=True)
    whole = whole.reshape(all_heads, DH, DH)

    places = jnp.arange(cat_query.shape[0], dtype=jnp.int32)
    causal = places[None, :] <= places[:, None]
    cat_inner = attend_inner(cat_query, cat_key, cat_value, causal, heads_here)
    rows = jnp.arange(resp_query.shape[0], dtype=jnp.int32)
    ends = jnp.cumsum(resp_lengths[0])
    segment = jnp.sum((rows[:, None] >= ends[None, :]).astype(jnp.int32), axis=1)
    mask = (segment[:, None] == segment[None, :]) & (rows[None, :] <= rows[:, None])
    resp_inner = attend_inner(resp_query, resp_key, resp_value, mask, all_heads)

    cat_raw = cat_inner + attend_outer(cat_query, prefix, heads_here)
    offset = lax.axis_index("resp") * (heads_here * DH)
    cat_gain = lax.dynamic_slice_in_dim(norm_gain, offset, heads_here * DH)
    cat_out = head_norm(cat_raw, cat_gain, heads_here)
    resp_raw = resp_inner + attend_outer(resp_query, whole, all_heads)
    resp_out = head_norm(resp_raw, norm_gain, all_heads)
    return (cat_out, resp_out)


def solution(mesh):
    placed = (
        P("seq", "resp"),
        P("seq", "resp"),
        P("seq", "resp"),
        P(("seq", "resp"), None),
        P(("seq", "resp"), None),
        P(("seq", "resp"), None),
        P(("seq", "resp"), None),
        P(),
    )
    return jax.shard_map(
        per_device,
        mesh=mesh,
        in_specs=placed,
        out_specs=(P("seq", "resp"), P(("seq", "resp"), None)),
        check_vma=False,
    )
```

```python
import jax
import jax.numpy as jnp
from jax import lax
from jax.sharding import PartitionSpec as P

DH = 128


def attend_inner(query, key, value, mask, heads):
    rows = query.shape[0]
    qh = query.reshape(rows, heads, DH)
    kh = key.reshape(rows, heads, DH)
    vh = value.reshape(rows, heads, DH)
    scores = jnp.einsum("thd,shd->hts", qh, kh, preferred_element_type=jnp.float32)
    scores = jnp.where(mask[None, :, :], scores, 0.0).astype(jnp.bfloat16)
    return jnp.einsum("hts,shd->thd", scores, vh, preferred_element_type=jnp.float32)


def attend_outer(query, state, heads):
    rows = query.shape[0]
    qh = query.reshape(rows, heads, DH).astype(jnp.float32)
    return jnp.einsum("thd,hde->the", qh, state, precision=lax.Precision.HIGHEST)


def block_state(key, value, heads):
    rows = key.shape[0]
    kh = key.reshape(rows, heads, DH)
    vh = value.reshape(rows, heads, DH)
    return jnp.einsum("shd,she->hde", kh, vh, preferred_element_type=jnp.float32)


def head_norm(raw, gain, heads):
    square = jnp.mean(raw * raw, axis=-1, keepdims=True)
    scaled = raw * lax.rsqrt(square + 1e-06) * gain.reshape(heads, DH)
    return scaled.reshape(raw.shape[0], heads * DH).astype(jnp.bfloat16)


def transpose_scan(local_state):
    peers = lax.axis_size("seq")
    chunks = local_state.reshape(peers, -1, DH)
    gathered = lax.all_to_all(chunks, "seq", 0, 0, tiled=True)
    before = lax.broadcasted_iota(jnp.int32, (peers, peers), 1) < lax.broadcasted_iota(
        jnp.int32, (peers, peers), 0
    )
    flat = gathered.reshape(peers, -1)
    exclusive = jnp.dot(
        before.astype(jnp.float32), flat, precision=lax.Precision.HIGHEST
    ).reshape(chunks.shape)
    prefix = lax.all_to_all(exclusive, "seq", 0, 0, tiled=True)
    return prefix.reshape(local_state.shape)


def per_device(
    cat_query, cat_key, cat_value, resp_query, resp_key, resp_value, resp_lengths, norm_gain
):
    heads_here = cat_query.shape[1] // DH
    all_heads = resp_query.shape[1] // DH
    local_state = block_state(cat_key, cat_value, heads_here)
    total = lax.psum(local_state, "seq")
    prefix = transpose_scan(local_state)
    whole = lax.all_gather(total, "resp", axis=0, tiled=True)

    places = jnp.arange(cat_query.shape[0], dtype=jnp.int32)
    causal = places[None, :] <= places[:, None]
    cat_inner = attend_inner(cat_query, cat_key, cat_value, causal, heads_here)
    rows = jnp.arange(resp_query.shape[0], dtype=jnp.int32)
    ends = jnp.cumsum(resp_lengths[0])
    segment = jnp.sum((rows[:, None] >= ends[None, :]).astype(jnp.int32), axis=1)
    mask = (segment[:, None] == segment[None, :]) & (rows[None, :] <= rows[:, None])
    resp_inner = attend_inner(resp_query, resp_key, resp_value, mask, all_heads)

    cat_raw = cat_inner + attend_outer(cat_query, prefix, heads_here)
    offset = lax.axis_index("resp") * (heads_here * DH)
    cat_gain = lax.dynamic_slice_in_dim(norm_gain, offset, heads_here * DH)
    cat_out = head_norm(cat_raw, cat_gain, heads_here)
    resp_raw = resp_inner + attend_outer(resp_query, whole, all_heads)
    resp_out = head_norm(resp_raw, norm_gain, all_heads)
    return (cat_out, resp_out)


def solution(mesh):
    placed = (
        P("seq", "resp"),
        P("seq", "resp"),
        P("seq", "resp"),
        P(("seq", "resp"), None),
        P(("seq", "resp"), None),
        P(("seq", "resp"), None),
        P(("seq", "resp"), None),
        P(),
    )
    return jax.shard_map(
        per_device,
        mesh=mesh,
        in_specs=placed,
        out_specs=(P("seq", "resp"), P(("seq", "resp"), None)),
        check_vma=False,
    )
```

```python
import jax
import jax.numpy as jnp
from jax import lax
from jax.sharding import PartitionSpec as P

DH = 128


def attend_inner(query, key, value, mask, heads):
    rows = query.shape[0]
    qh = query.reshape(rows, heads, DH)
    kh = key.reshape(rows, heads, DH)
    vh = value.reshape(rows, heads, DH)
    scores = jnp.einsum("thd,shd->hts", qh, kh, preferred_element_type=jnp.float32)
    scores = jnp.where(mask[None, :, :], scores, 0.0).astype(jnp.bfloat16)
    return jnp.einsum("hts,shd->thd", scores, vh, preferred_element_type=jnp.float32)


def attend_outer(query, state, heads):
    rows = query.shape[0]
    qh = query.reshape(rows, heads, DH).astype(jnp.float32)
    return jnp.einsum("thd,hde->the", qh, state, precision=lax.Precision.HIGHEST)


def block_state(key, value, heads):
    rows = key.shape[0]
    kh = key.reshape(rows, heads, DH)
    vh = value.reshape(rows, heads, DH)
    return jnp.einsum("shd,she->hde", kh, vh, preferred_element_type=jnp.float32)


def head_norm(raw, gain, heads):
    square = jnp.mean(raw * raw, axis=-1, keepdims=True)
    scaled = raw * lax.rsqrt(square + 1e-06) * gain.reshape(heads, DH)
    return scaled.reshape(raw.shape[0], heads * DH).astype(jnp.bfloat16)


def transpose_scan(local_state):
    peers = lax.axis_size("seq")
    chunks = local_state.reshape(peers, -1, DH)
    gathered = lax.all_to_all(chunks, "seq", 0, 0, tiled=True)
    before = lax.broadcasted_iota(jnp.int32, (peers, peers), 1) < lax.broadcasted_iota(
        jnp.int32, (peers, peers), 0
    )
    flat = gathered.reshape(peers, -1)
    exclusive = jnp.dot(
        before.astype(jnp.float32), flat, precision=lax.Precision.HIGHEST
    ).reshape(chunks.shape)
    total = jnp.sum(gathered, axis=0, keepdims=True)
    payload = jnp.concatenate([exclusive, jnp.broadcast_to(total, chunks.shape)], axis=1)
    back = lax.all_to_all(payload, "seq", 0, 0, tiled=True)
    half = chunks.shape[1]
    prefix = back[:, :half].reshape(local_state.shape)
    total = back[:, half:].reshape(local_state.shape)
    return prefix, total


def per_device(
    cat_query, cat_key, cat_value, resp_query, resp_key, resp_value, resp_lengths, norm_gain
):
    heads_here = cat_query.shape[1] // DH
    all_heads = resp_query.shape[1] // DH
    local_state = block_state(cat_key, cat_value, heads_here)
    prefix, total = transpose_scan(local_state)
    other = lax.ppermute(total, "resp", [(0, 1), (1, 0)])
    first = lax.axis_index("resp") == 0
    whole = jnp.concatenate(
        [jnp.where(first, total, other), jnp.where(first, other, total)], axis=0
    )

    places = jnp.arange(cat_query.shape[0], dtype=jnp.int32)
    causal = places[None, :] <= places[:, None]
    cat_inner = attend_inner(cat_query, cat_key, cat_value, causal, heads_here)
    rows = jnp.arange(resp_query.shape[0], dtype=jnp.int32)
    ends = jnp.cumsum(resp_lengths[0])
    segment = jnp.sum((rows[:, None] >= ends[None, :]).astype(jnp.int32), axis=1)
    mask = (segment[:, None] == segment[None, :]) & (rows[None, :] <= rows[:, None])
    resp_inner = attend_inner(resp_query, resp_key, resp_value, mask, all_heads)

    cat_raw = cat_inner + attend_outer(cat_query, prefix, heads_here)
    offset = lax.axis_index("resp") * (heads_here * DH)
    cat_gain = lax.dynamic_slice_in_dim(norm_gain, offset, heads_here * DH)
    cat_out = head_norm(cat_raw, cat_gain, heads_here)
    resp_raw = resp_inner + attend_outer(resp_query, whole, all_heads)
    resp_out = head_norm(resp_raw, norm_gain, all_heads)
    return (cat_out, resp_out)


def solution(mesh):
    placed = (
        P("seq", "resp"),
        P("seq", "resp"),
        P("seq", "resp"),
        P(("seq", "resp"), None),
        P(("seq", "resp"), None),
        P(("seq", "resp"), None),
        P(("seq", "resp"), None),
        P(),
    )
    return jax.shard_map(
        per_device,
        mesh=mesh,
        in_specs=placed,
        out_specs=(P("seq", "resp"), P(("seq", "resp"), None)),
        check_vma=False,
    )
```

```python
import jax
import jax.numpy as jnp
from jax import lax
from jax.experimental import pallas as pl
from jax.experimental.pallas import tpu as pltpu
from jax.sharding import PartitionSpec as P

DH = 128


def attend_inner(query, key, value, mask, heads):
    rows = query.shape[0]
    qh = query.reshape(rows, heads, DH)
    kh = key.reshape(rows, heads, DH)
    vh = value.reshape(rows, heads, DH)
    scores = jnp.einsum("thd,shd->hts", qh, kh, preferred_element_type=jnp.float32)
    scores = jnp.where(mask[None, :, :], scores, 0.0).astype(jnp.bfloat16)
    return jnp.einsum("hts,shd->thd", scores, vh, preferred_element_type=jnp.float32)


def attend_outer(query, state, heads):
    rows = query.shape[0]
    qh = query.reshape(rows, heads, DH).astype(jnp.float32)
    return jnp.einsum("thd,hde->the", qh, state, precision=lax.Precision.HIGHEST)


def block_state(key, value, heads):
    rows = key.shape[0]
    kh = key.reshape(rows, heads, DH)
    vh = value.reshape(rows, heads, DH)
    return jnp.einsum("shd,she->hde", kh, vh, preferred_element_type=jnp.float32)


def head_norm(raw, gain, heads):
    square = jnp.mean(raw * raw, axis=-1, keepdims=True)
    scaled = raw * lax.rsqrt(square + 1e-06) * gain.reshape(heads, DH)
    return scaled.reshape(raw.shape[0], heads * DH).astype(jnp.bfloat16)


def scan_kernel(x_ref, out_ref, got, payload, back, sends, recvs):
    peers, half = x_ref.shape[0], x_ref.shape[1]
    me = lax.axis_index("seq")
    mesh_ids = pl.DeviceIdType.MESH

    def exchange(phase, src, dst):
        def copy_to(peer, at):
            return pltpu.make_async_remote_copy(
                src_ref=src.at[peer],
                dst_ref=dst.at[at],
                send_sem=sends.at[phase],
                recv_sem=recvs.at[phase],
                device_id={"seq": peer},
                device_id_type=mesh_ids,
            )

        def start(t, carry):
            copy_to(lax.rem(me + t, peers), me).start()
            return carry

        lax.fori_loop(1, peers, start, 0)
        dst[pl.ds(me, 1)] = src[pl.ds(me, 1)]

        others = pl.ds(0, peers - 1)
        everyone = pltpu.make_async_remote_copy(
            src_ref=src.at[others],
            dst_ref=dst.at[others],
            send_sem=sends.at[phase],
            recv_sem=recvs.at[phase],
            device_id={"seq": lax.rem(me + 1, peers)},
            device_id_type=mesh_ids,
        )
        everyone.wait_send()
        everyone.wait_recv()

    exchange(0, x_ref, got)

    def running(j, acc):
        payload[pl.ds(j, 1), pl.ds(0, half), :] = acc[None]
        return acc + got[j]

    total = lax.fori_loop(0, peers, running, jnp.zeros((half, DH), jnp.float32), unroll=8)

    def fill(j, carry):
        payload[pl.ds(j, 1), pl.ds(half, half), :] = total[None]
        return carry

    lax.fori_loop(0, peers, fill, 0, unroll=8)
    exchange(1, payload, back)
    out_ref[...] = back[...]


def transpose_scan(local_state):
    peers = lax.axis_size("seq")
    chunks = local_state.reshape(peers, -1, DH)
    half = chunks.shape[1]
    vmem = pl.BlockSpec(memory_space=pltpu.VMEM)
    back = pl.pallas_call(
        scan_kernel,
        out_shape=jax.ShapeDtypeStruct((peers, 2 * half, DH), jnp.float32),
        in_specs=[vmem],
        out_specs=vmem,
        scratch_shapes=[
            pltpu.VMEM((peers, half, DH), jnp.float32),
            pltpu.VMEM((peers, 2 * half, DH), jnp.float32),
            pltpu.VMEM((peers, 2 * half, DH), jnp.float32),
            pltpu.SemaphoreType.DMA((2,)),
            pltpu.SemaphoreType.DMA((2,)),
        ],
        compiler_params=pltpu.CompilerParams(has_side_effects=True),
        cost_estimate=pl.CostEstimate(
            flops=2 * peers * half * DH, transcendentals=0, bytes_accessed=12 * peers * half * DH
        ),
    )(chunks)
    prefix = back[:, :half].reshape(local_state.shape)
    total = back[:, half:].reshape(local_state.shape)
    return prefix, total


def per_device(
    cat_query, cat_key, cat_value, resp_query, resp_key, resp_value, resp_lengths, norm_gain
):
    heads_here = cat_query.shape[1] // DH
    all_heads = resp_query.shape[1] // DH
    local_state = block_state(cat_key, cat_value, heads_here)
    prefix, total = transpose_scan(local_state)
    other = lax.ppermute(total, "resp", [(0, 1), (1, 0)])
    first = lax.axis_index("resp") == 0
    whole = jnp.concatenate(
        [jnp.where(first, total, other), jnp.where(first, other, total)], axis=0
    )

    places = jnp.arange(cat_query.shape[0], dtype=jnp.int32)
    causal = places[None, :] <= places[:, None]
    cat_inner = attend_inner(cat_query, cat_key, cat_value, causal, heads_here)
    rows = jnp.arange(resp_query.shape[0], dtype=jnp.int32)
    ends = jnp.cumsum(resp_lengths[0])
    segment = jnp.sum((rows[:, None] >= ends[None, :]).astype(jnp.int32), axis=1)
    mask = (segment[:, None] == segment[None, :]) & (rows[None, :] <= rows[:, None])
    resp_inner = attend_inner(resp_query, resp_key, resp_value, mask, all_heads)

    cat_raw = cat_inner + attend_outer(cat_query, prefix, heads_here)
    offset = lax.axis_index("resp") * (heads_here * DH)
    cat_gain = lax.dynamic_slice_in_dim(norm_gain, offset, heads_here * DH)
    cat_out = head_norm(cat_raw, cat_gain, heads_here)
    resp_raw = resp_inner + attend_outer(resp_query, whole, all_heads)
    resp_out = head_norm(resp_raw, norm_gain, all_heads)
    return (cat_out, resp_out)


def solution(mesh):
    placed = (
        P("seq", "resp"),
        P("seq", "resp"),
        P("seq", "resp"),
        P(("seq", "resp"), None),
        P(("seq", "resp"), None),
        P(("seq", "resp"), None),
        P(("seq", "resp"), None),
        P(),
    )
    return jax.shard_map(
        per_device,
        mesh=mesh,
        in_specs=placed,
        out_specs=(P("seq", "resp"), P(("seq", "resp"), None)),
        check_vma=False,
    )
```

```python
import jax
import jax.numpy as jnp
from jax import lax
from jax.experimental import pallas as pl
from jax.experimental.pallas import tpu as pltpu
from jax.sharding import PartitionSpec as P

DH = 128


def attend_inner(query, key, value, mask, heads):
    rows = query.shape[0]
    qh = query.reshape(rows, heads, DH)
    kh = key.reshape(rows, heads, DH)
    vh = value.reshape(rows, heads, DH)
    scores = jnp.einsum("thd,shd->hts", qh, kh, preferred_element_type=jnp.float32)
    scores = jnp.where(mask[None, :, :], scores, 0.0).astype(jnp.bfloat16)
    return jnp.einsum("hts,shd->thd", scores, vh, preferred_element_type=jnp.float32)


def attend_outer(query, state, heads):
    rows = query.shape[0]
    qh = query.reshape(rows, heads, DH).astype(jnp.float32)
    return jnp.einsum("thd,hde->the", qh, state, precision=lax.Precision.HIGHEST)


def block_state(key, value, heads):
    rows = key.shape[0]
    kh = key.reshape(rows, heads, DH)
    vh = value.reshape(rows, heads, DH)
    return jnp.einsum("shd,she->hde", kh, vh, preferred_element_type=jnp.float32)


def head_norm(raw, gain, heads):
    square = jnp.mean(raw * raw, axis=-1, keepdims=True)
    scaled = raw * lax.rsqrt(square + 1e-06) * gain.reshape(heads, DH)
    return scaled.reshape(raw.shape[0], heads * DH).astype(jnp.bfloat16)


def scan_kernel(x_ref, out_ref, got, payload, back, sends, recvs):
    peers, half = x_ref.shape[0], x_ref.shape[1]
    me = lax.axis_index("seq")
    mesh_ids = pl.DeviceIdType.MESH

    def exchange(phase, src, dst):
        def copy_to(peer, at):
            return pltpu.make_async_remote_copy(
                src_ref=src.at[peer],
                dst_ref=dst.at[at],
                send_sem=sends.at[phase],
                recv_sem=recvs.at[phase],
                device_id={"seq": peer},
                device_id_type=mesh_ids,
            )

        def start(i, carry):
            t = jnp.where(i % 2 == 1, (i + 1) // 2, peers - i // 2)
            copy_to(lax.rem(me + t, peers), me).start()
            return carry

        lax.fori_loop(1, peers, start, 0)
        dst[pl.ds(me, 1)] = src[pl.ds(me, 1)]

        others = pl.ds(0, peers - 1)
        everyone = pltpu.make_async_remote_copy(
            src_ref=src.at[others],
            dst_ref=dst.at[others],
            send_sem=sends.at[phase],
            recv_sem=recvs.at[phase],
            device_id={"seq": lax.rem(me + 1, peers)},
            device_id_type=mesh_ids,
        )
        everyone.wait_send()
        everyone.wait_recv()

    exchange(0, x_ref, got)

    def running(j, acc):
        payload[pl.ds(j, 1), pl.ds(0, half), :] = acc[None]
        return acc + got[j]

    total = lax.fori_loop(0, peers, running, jnp.zeros((half, DH), jnp.float32), unroll=8)

    def fill(j, carry):
        payload[pl.ds(j, 1), pl.ds(half, half), :] = total[None]
        return carry

    lax.fori_loop(0, peers, fill, 0, unroll=8)
    exchange(1, payload, back)
    out_ref[...] = back[...]


def transpose_scan(local_state):
    peers = lax.axis_size("seq")
    chunks = local_state.reshape(peers, -1, DH)
    half = chunks.shape[1]
    vmem = pl.BlockSpec(memory_space=pltpu.VMEM)
    back = pl.pallas_call(
        scan_kernel,
        out_shape=jax.ShapeDtypeStruct((peers, 2 * half, DH), jnp.float32),
        in_specs=[vmem],
        out_specs=vmem,
        scratch_shapes=[
            pltpu.VMEM((peers, half, DH), jnp.float32),
            pltpu.VMEM((peers, 2 * half, DH), jnp.float32),
            pltpu.VMEM((peers, 2 * half, DH), jnp.float32),
            pltpu.SemaphoreType.DMA((2,)),
            pltpu.SemaphoreType.DMA((2,)),
        ],
        compiler_params=pltpu.CompilerParams(has_side_effects=True),
        cost_estimate=pl.CostEstimate(
            flops=2 * peers * half * DH, transcendentals=0, bytes_accessed=12 * peers * half * DH
        ),
    )(chunks)
    prefix = back[:, :half].reshape(local_state.shape)
    total = back[:, half:].reshape(local_state.shape)
    return prefix, total


def per_device(
    cat_query, cat_key, cat_value, resp_query, resp_key, resp_value, resp_lengths, norm_gain
):
    heads_here = cat_query.shape[1] // DH
    all_heads = resp_query.shape[1] // DH
    local_state = block_state(cat_key, cat_value, heads_here)
    prefix, total = transpose_scan(local_state)
    other = lax.ppermute(total, "resp", [(0, 1), (1, 0)])
    first = lax.axis_index("resp") == 0
    whole = jnp.concatenate(
        [jnp.where(first, total, other), jnp.where(first, other, total)], axis=0
    )

    places = jnp.arange(cat_query.shape[0], dtype=jnp.int32)
    causal = places[None, :] <= places[:, None]
    cat_inner = attend_inner(cat_query, cat_key, cat_value, causal, heads_here)
    rows = jnp.arange(resp_query.shape[0], dtype=jnp.int32)
    ends = jnp.cumsum(resp_lengths[0])
    segment = jnp.sum((rows[:, None] >= ends[None, :]).astype(jnp.int32), axis=1)
    mask = (segment[:, None] == segment[None, :]) & (rows[None, :] <= rows[:, None])
    resp_inner = attend_inner(resp_query, resp_key, resp_value, mask, all_heads)

    cat_raw = cat_inner + attend_outer(cat_query, prefix, heads_here)
    offset = lax.axis_index("resp") * (heads_here * DH)
    cat_gain = lax.dynamic_slice_in_dim(norm_gain, offset, heads_here * DH)
    cat_out = head_norm(cat_raw, cat_gain, heads_here)
    resp_raw = resp_inner + attend_outer(resp_query, whole, all_heads)
    resp_out = head_norm(resp_raw, norm_gain, all_heads)
    return (cat_out, resp_out)


def solution(mesh):
    placed = (
        P("seq", "resp"),
        P("seq", "resp"),
        P("seq", "resp"),
        P(("seq", "resp"), None),
        P(("seq", "resp"), None),
        P(("seq", "resp"), None),
        P(("seq", "resp"), None),
        P(),
    )
    return jax.shard_map(
        per_device,
        mesh=mesh,
        in_specs=placed,
        out_specs=(P("seq", "resp"), P(("seq", "resp"), None)),
        check_vma=False,
    )
```

```python
import jax
import jax.numpy as jnp
from jax import lax
from jax.experimental import pallas as pl
from jax.experimental.pallas import tpu as pltpu
from jax.sharding import PartitionSpec as P

DH = 128


def attend_inner(query, key, value, mask, heads):
    rows = query.shape[0]
    qh = query.reshape(rows, heads, DH)
    kh = key.reshape(rows, heads, DH)
    vh = value.reshape(rows, heads, DH)
    scores = jnp.einsum("thd,shd->hts", qh, kh, preferred_element_type=jnp.float32)
    scores = jnp.where(mask[None, :, :], scores, 0.0).astype(jnp.bfloat16)
    return jnp.einsum("hts,shd->thd", scores, vh, preferred_element_type=jnp.float32)


def attend_outer(query, state, heads):
    rows = query.shape[0]
    qh = query.reshape(rows, heads, DH).astype(jnp.float32)
    return jnp.einsum("thd,hde->the", qh, state, precision=lax.Precision.HIGHEST)


def block_state(key, value, heads):
    rows = key.shape[0]
    kh = key.reshape(rows, heads, DH)
    vh = value.reshape(rows, heads, DH)
    return jnp.einsum("shd,she->hde", kh, vh, preferred_element_type=jnp.float32)


def head_norm(raw, gain, heads):
    square = jnp.mean(raw * raw, axis=-1, keepdims=True)
    scaled = raw * lax.rsqrt(square + 1e-06) * gain.reshape(heads, DH)
    return scaled.reshape(raw.shape[0], heads * DH).astype(jnp.bfloat16)


def heads_inner(q_ref, k_ref, v_ref, keep, o_ref):
    def one(h, carry):
        cols = pl.ds(pl.multiple_of(h * DH, DH), DH)
        scores = lax.dot_general(
            q_ref[:, cols], k_ref[:, cols], (((1,), (1,)), ((), ())),
            preferred_element_type=jnp.float32,
        )
        scores = jnp.where(keep, scores, 0.0).astype(jnp.bfloat16)
        o_ref[:, cols] = jnp.dot(scores, v_ref[:, cols], preferred_element_type=jnp.float32)
        return carry

    lax.fori_loop(0, q_ref.shape[1] // DH, one, 0)


def scan_kernel(
    x_ref, cq, ck, cv, rq, rk, rv, rmask, out_ref, cat_ref, resp_ref, got, payload, back, sends, recvs
):
    peers, half = x_ref.shape[0], x_ref.shape[1]
    me = lax.axis_index("seq")
    mesh_ids = pl.DeviceIdType.MESH

    def exchange(phase, src, dst):
        def copy_to(peer, at):
            return pltpu.make_async_remote_copy(
                src_ref=src.at[peer],
                dst_ref=dst.at[at],
                send_sem=sends.at[phase],
                recv_sem=recvs.at[phase],
                device_id={"seq": peer},
                device_id_type=mesh_ids,
            )

        def start(t, carry):
            copy_to(lax.rem(me + t, peers), me).start()
            return carry

        lax.fori_loop(1, peers, start, 0)
        dst[pl.ds(me, 1)] = src[pl.ds(me, 1)]
        if phase == 0:
            rows = lax.broadcasted_iota(jnp.int32, (cq.shape[0], cq.shape[0]), 0)
            cols = lax.broadcasted_iota(jnp.int32, (cq.shape[0], cq.shape[0]), 1)
            heads_inner(cq, ck, cv, cols <= rows, cat_ref)
        else:
            heads_inner(rq, rk, rv, rmask[...] != 0, resp_ref)

        others = pl.ds(0, peers - 1)
        everyone = pltpu.make_async_remote_copy(
            src_ref=src.at[others],
            dst_ref=dst.at[others],
            send_sem=sends.at[phase],
            recv_sem=recvs.at[phase],
            device_id={"seq": lax.rem(me + 1, peers)},
            device_id_type=mesh_ids,
        )
        everyone.wait_send()
        everyone.wait_recv()

    exchange(0, x_ref, got)

    def running(j, acc):
        payload[pl.ds(j, 1), pl.ds(0, half), :] = acc[None]
        return acc + got[j]

    total = lax.fori_loop(0, peers, running, jnp.zeros((half, DH), jnp.float32), unroll=8)

    def fill(j, carry):
        payload[pl.ds(j, 1), pl.ds(half, half), :] = total[None]
        return carry

    lax.fori_loop(0, peers, fill, 0, unroll=8)
    exchange(1, payload, back)
    out_ref[...] = back[...]


def transpose_scan(local_state, cat, resp, rmask):
    peers = lax.axis_size("seq")
    chunks = local_state.reshape(peers, -1, DH)
    half = chunks.shape[1]
    vmem = pl.BlockSpec(memory_space=pltpu.VMEM)
    back, cat_inner, resp_inner = pl.pallas_call(
        scan_kernel,
        out_shape=(
            jax.ShapeDtypeStruct((peers, 2 * half, DH), jnp.float32),
            jax.ShapeDtypeStruct(cat[0].shape, jnp.float32),
            jax.ShapeDtypeStruct(resp[0].shape, jnp.float32),
        ),
        in_specs=[vmem] * 8,
        out_specs=(vmem, vmem, vmem),
        scratch_shapes=[
            pltpu.VMEM((peers, half, DH), jnp.float32),
            pltpu.VMEM((peers, 2 * half, DH), jnp.float32),
            pltpu.VMEM((peers, 2 * half, DH), jnp.float32),
            pltpu.SemaphoreType.DMA((2,)),
            pltpu.SemaphoreType.DMA((2,)),
        ],
        compiler_params=pltpu.CompilerParams(has_side_effects=True),
        cost_estimate=pl.CostEstimate(
            flops=4 * DH * (cat[0].shape[0] * cat[0].shape[1] + resp[0].shape[0] * resp[0].shape[1]),
            transcendentals=0,
            bytes_accessed=12 * peers * half * DH,
        ),
    )(chunks, *cat, *resp, rmask)
    prefix = back[:, :half].reshape(local_state.shape)
    total = back[:, half:].reshape(local_state.shape)
    return prefix, total, cat_inner, resp_inner


def per_device(
    cat_query, cat_key, cat_value, resp_query, resp_key, resp_value, resp_lengths, norm_gain
):
    heads_here = cat_query.shape[1] // DH
    all_heads = resp_query.shape[1] // DH
    local_state = block_state(cat_key, cat_value, heads_here)
    rows = jnp.arange(resp_query.shape[0], dtype=jnp.int32)
    ends = jnp.cumsum(resp_lengths[0])
    segment = jnp.sum((rows[:, None] >= ends[None, :]).astype(jnp.int32), axis=1)
    mask = (segment[:, None] == segment[None, :]) & (rows[None, :] <= rows[:, None])
    prefix, total, cat_inner, resp_inner = transpose_scan(
        local_state,
        (cat_query, cat_key, cat_value),
        (resp_query, resp_key, resp_value),
        mask.astype(jnp.int32),
    )
    other = lax.ppermute(total, "resp", [(0, 1), (1, 0)])
    first = lax.axis_index("resp") == 0
    whole = jnp.concatenate(
        [jnp.where(first, total, other), jnp.where(first, other, total)], axis=0
    )

    cat_raw = cat_inner.reshape(-1, heads_here, DH) + attend_outer(cat_query, prefix, heads_here)
    offset = lax.axis_index("resp") * (heads_here * DH)
    cat_gain = lax.dynamic_slice_in_dim(norm_gain, offset, heads_here * DH)
    cat_out = head_norm(cat_raw, cat_gain, heads_here)
    resp_raw = resp_inner.reshape(-1, all_heads, DH) + attend_outer(resp_query, whole, all_heads)
    resp_out = head_norm(resp_raw, norm_gain, all_heads)
    return (cat_out, resp_out)


def solution(mesh):
    placed = (
        P("seq", "resp"),
        P("seq", "resp"),
        P("seq", "resp"),
        P(("seq", "resp"), None),
        P(("seq", "resp"), None),
        P(("seq", "resp"), None),
        P(("seq", "resp"), None),
        P(),
    )
    return jax.shard_map(
        per_device,
        mesh=mesh,
        in_specs=placed,
        out_specs=(P("seq", "resp"), P(("seq", "resp"), None)),
        check_vma=False,
    )
```

```python
import jax
import jax.numpy as jnp
from jax import lax
from jax.experimental import pallas as pl
from jax.experimental.pallas import tpu as pltpu
from jax.sharding import PartitionSpec as P

DH = 128


def block_state(key, value, heads):
    rows = key.shape[0]
    kh = key.reshape(rows, heads, DH)
    vh = value.reshape(rows, heads, DH)
    return jnp.einsum("shd,she->hde", kh, vh, preferred_element_type=jnp.float32)


def heads_inner(q_ref, k_ref, v_ref, keep, o_ref):
    def one(h, carry):
        cols = pl.ds(pl.multiple_of(h * DH, DH), DH)
        scores = lax.dot_general(
            q_ref[:, cols], k_ref[:, cols], (((1,), (1,)), ((), ())),
            preferred_element_type=jnp.float32,
        )
        scores = jnp.where(keep, scores, 0.0).astype(jnp.bfloat16)
        o_ref[:, cols] = jnp.dot(scores, v_ref[:, cols], preferred_element_type=jnp.float32)
        return carry

    lax.fori_loop(0, q_ref.shape[1] // DH, one, 0)


def split_dot(q, state):
    hi = state.astype(jnp.bfloat16)
    rest = state - hi.astype(jnp.float32)
    mid = rest.astype(jnp.bfloat16)
    lo = (rest - mid.astype(jnp.float32)).astype(jnp.bfloat16)
    acc = jnp.dot(q, hi, preferred_element_type=jnp.float32)
    acc = acc + jnp.dot(q, mid, preferred_element_type=jnp.float32)
    return acc + jnp.dot(q, lo, preferred_element_type=jnp.float32)


def head_state(ref, h, first, half):
    if half <= DH:
        group = DH // half
        return ref[pl.ds(h * group, group), pl.ds(first, half), :].reshape(DH, DH)
    per = half // DH
    return ref[h // per, pl.ds(first + (h % per) * DH, DH), :]


def heads_finish(q_ref, inner_ref, state_of, gain_ref, gain_at, o_ref):
    def one(h, carry):
        cols = pl.ds(pl.multiple_of(h * DH, DH), DH)
        raw = inner_ref[:, cols] + split_dot(q_ref[:, cols], state_of(h))
        square = jnp.mean(raw * raw, axis=-1, keepdims=True)
        gain = gain_ref[:, pl.ds(pl.multiple_of(gain_at + h * DH, DH), DH)]
        o_ref[:, cols] = (raw * lax.rsqrt(square + 1e-06) * gain).astype(o_ref.dtype)
        return carry

    lax.fori_loop(0, q_ref.shape[1] // DH, one, 0)


def layer_kernel(
    x_ref, cq, ck, cv, rq, rk, rv, rmask, gain_ref,
    cat_out, resp_out,
    got, payload, back, whole, cat_inner, resp_inner, sends, recvs,
):
    peers, half = x_ref.shape[0], x_ref.shape[1]
    me = lax.axis_index("seq")
    side = lax.axis_index("resp")
    mesh_ids = pl.DeviceIdType.MESH

    def exchange(phase, src, dst, cover):
        def copy_to(peer, at):
            return pltpu.make_async_remote_copy(
                src_ref=src.at[peer],
                dst_ref=dst.at[at],
                send_sem=sends.at[phase],
                recv_sem=recvs.at[phase],
                device_id={"seq": peer},
                device_id_type=mesh_ids,
            )

        def start(t, carry):
            copy_to(lax.rem(me + t, peers), me).start()
            return carry

        lax.fori_loop(1, peers, start, 0)
        dst[pl.ds(me, 1)] = src[pl.ds(me, 1)]
        cover()
        others = pl.ds(0, peers - 1)
        everyone = pltpu.make_async_remote_copy(
            src_ref=src.at[others],
            dst_ref=dst.at[others],
            send_sem=sends.at[phase],
            recv_sem=recvs.at[phase],
            device_id={"seq": lax.rem(me + 1, peers)},
            device_id_type=mesh_ids,
        )
        everyone.wait_send()
        everyone.wait_recv()

    def cat_cover():
        rows = lax.broadcasted_iota(jnp.int32, (cq.shape[0], cq.shape[0]), 0)
        cols = lax.broadcasted_iota(jnp.int32, (cq.shape[0], cq.shape[0]), 1)
        heads_inner(cq, ck, cv, cols <= rows, cat_inner)

    def resp_cover():
        heads_inner(rq, rk, rv, rmask[...] != 0, resp_inner)

    exchange(0, x_ref, got, cat_cover)

    def running(j, acc):
        payload[pl.ds(j, 1), pl.ds(0, half), :] = acc[None]
        return acc + got[j]

    total = lax.fori_loop(0, peers, running, jnp.zeros((half, DH), jnp.float32), unroll=8)

    def fill(j, carry):
        payload[pl.ds(j, 1), pl.ds(half, half), :] = total[None]
        return carry

    lax.fori_loop(0, peers, fill, 0, unroll=8)
    exchange(1, payload, back, resp_cover)

    partner = pltpu.make_async_remote_copy(
        src_ref=back.at[:, pl.ds(half, half)],
        dst_ref=whole.at[pl.ds(side * peers, peers)],
        send_sem=sends.at[2],
        recv_sem=recvs.at[2],
        device_id={"resp": 1 - side},
        device_id_type=mesh_ids,
    )
    partner.start()
    whole[pl.ds(side * peers, peers)] = back[:, pl.ds(half, half)]

    def prefix_of(h):
        return head_state(back, h, 0, half)

    heads_finish(cq, cat_inner, prefix_of, gain_ref, side * cq.shape[1], cat_out)
    partner.wait_send()
    arrived = pltpu.make_async_remote_copy(
        src_ref=back.at[:, pl.ds(half, half)],
        dst_ref=whole.at[pl.ds((1 - side) * peers, peers)],
        send_sem=sends.at[2],
        recv_sem=recvs.at[2],
        device_id={"resp": 1 - side},
        device_id_type=mesh_ids,
    )
    arrived.wait_recv()

    def total_of(h):
        return head_state(whole, h, 0, half)

    heads_finish(rq, resp_inner, total_of, gain_ref, 0, resp_out)


def layer(local_state, cat, resp, rmask, gain):
    peers = lax.axis_size("seq")
    chunks = local_state.reshape(peers, -1, DH)
    half = chunks.shape[1]
    vmem = pl.BlockSpec(memory_space=pltpu.VMEM)
    cat_rows, cat_width = cat[0].shape
    resp_rows, resp_width = resp[0].shape
    return pl.pallas_call(
        layer_kernel,
        out_shape=(
            jax.ShapeDtypeStruct(cat[0].shape, jnp.bfloat16),
            jax.ShapeDtypeStruct(resp[0].shape, jnp.bfloat16),
        ),
        in_specs=[vmem] * 9,
        out_specs=(vmem, vmem),
        scratch_shapes=[
            pltpu.VMEM((peers, half, DH), jnp.float32),
            pltpu.VMEM((peers, 2 * half, DH), jnp.float32),
            pltpu.VMEM((peers, 2 * half, DH), jnp.float32),
            pltpu.VMEM((2 * peers, half, DH), jnp.float32),
            pltpu.VMEM(cat[0].shape, jnp.float32),
            pltpu.VMEM(resp[0].shape, jnp.float32),
            pltpu.SemaphoreType.DMA((3,)),
            pltpu.SemaphoreType.DMA((3,)),
        ],
        compiler_params=pltpu.CompilerParams(has_side_effects=True),
        cost_estimate=pl.CostEstimate(
            flops=10 * DH * (cat_rows * cat_width + resp_rows * resp_width),
            transcendentals=cat_rows * cat_width // DH + resp_rows * resp_width // DH,
            bytes_accessed=14 * peers * half * DH,
        ),
    )(chunks, *cat, *resp, rmask, gain)


def per_device(
    cat_query, cat_key, cat_value, resp_query, resp_key, resp_value, resp_lengths, norm_gain
):
    heads_here = cat_query.shape[1] // DH
    local_state = block_state(cat_key, cat_value, heads_here)
    rows = jnp.arange(resp_query.shape[0], dtype=jnp.int32)
    ends = jnp.cumsum(resp_lengths[0])
    segment = jnp.sum((rows[:, None] >= ends[None, :]).astype(jnp.int32), axis=1)
    mask = (segment[:, None] == segment[None, :]) & (rows[None, :] <= rows[:, None])
    return layer(
        local_state,
        (cat_query, cat_key, cat_value),
        (resp_query, resp_key, resp_value),
        mask.astype(jnp.int32),
        norm_gain.reshape(1, -1),
    )


def solution(mesh):
    placed = (
        P("seq", "resp"),
        P("seq", "resp"),
        P("seq", "resp"),
        P(("seq", "resp"), None),
        P(("seq", "resp"), None),
        P(("seq", "resp"), None),
        P(("seq", "resp"), None),
        P(),
    )
    return jax.shard_map(
        per_device,
        mesh=mesh,
        in_specs=placed,
        out_specs=(P("seq", "resp"), P(("seq", "resp"), None)),
        check_vma=False,
    )
```

```python
import jax
import jax.numpy as jnp
from jax import lax
from jax.experimental import pallas as pl
from jax.experimental.pallas import tpu as pltpu
from jax.sharding import PartitionSpec as P

DH = 128
UNROLL = 4


def block_state(key, value, heads):
    rows = key.shape[0]
    kh = key.reshape(rows, heads, DH)
    vh = value.reshape(rows, heads, DH)
    return jnp.einsum("shd,she->hde", kh, vh, preferred_element_type=jnp.float32)


def heads_inner(q_ref, k_ref, v_ref, keep, o_ref):
    def one(h, carry):
        cols = pl.ds(pl.multiple_of(h * DH, DH), DH)
        scores = lax.dot_general(
            q_ref[:, cols], k_ref[:, cols], (((1,), (1,)), ((), ())),
            preferred_element_type=jnp.float32,
        )
        scores = jnp.where(keep, scores, 0.0).astype(jnp.bfloat16)
        o_ref[:, cols] = jnp.dot(scores, v_ref[:, cols], preferred_element_type=jnp.float32)
        return carry

    lax.fori_loop(0, q_ref.shape[1] // DH, one, 0, unroll=UNROLL)


def split_dot(q, state):
    hi = state.astype(jnp.bfloat16)
    rest = state - hi.astype(jnp.float32)
    mid = rest.astype(jnp.bfloat16)
    lo = (rest - mid.astype(jnp.float32)).astype(jnp.bfloat16)
    acc = jnp.dot(q, hi, preferred_element_type=jnp.float32)
    acc = acc + jnp.dot(q, mid, preferred_element_type=jnp.float32)
    return acc + jnp.dot(q, lo, preferred_element_type=jnp.float32)


def head_state(ref, h, first, half):
    if half <= DH:
        group = DH // half
        return ref[pl.ds(h * group, group), pl.ds(first, half), :].reshape(DH, DH)
    per = half // DH
    return ref[h // per, pl.ds(first + (h % per) * DH, DH), :]


def heads_finish(q_ref, inner_ref, state_of, gain_ref, gain_at, o_ref):
    def one(h, carry):
        cols = pl.ds(pl.multiple_of(h * DH, DH), DH)
        raw = inner_ref[:, cols] + split_dot(q_ref[:, cols], state_of(h))
        square = jnp.mean(raw * raw, axis=-1, keepdims=True)
        gain = gain_ref[:, pl.ds(pl.multiple_of(gain_at + h * DH, DH), DH)]
        o_ref[:, cols] = (raw * lax.rsqrt(square + 1e-06) * gain).astype(o_ref.dtype)
        return carry

    lax.fori_loop(0, q_ref.shape[1] // DH, one, 0, unroll=UNROLL)


def layer_kernel(
    x_ref, cq, ck, cv, rq, rk, rv, rmask, gain_ref,
    cat_out, resp_out,
    got, payload, back, whole, cat_inner, resp_inner, sends, recvs,
):
    peers, half = x_ref.shape[0], x_ref.shape[1]
    me = lax.axis_index("seq")
    side = lax.axis_index("resp")
    mesh_ids = pl.DeviceIdType.MESH

    def exchange(phase, src, dst, cover):
        def copy_to(peer, at):
            return pltpu.make_async_remote_copy(
                src_ref=src.at[peer],
                dst_ref=dst.at[at],
                send_sem=sends.at[phase],
                recv_sem=recvs.at[phase],
                device_id={"seq": peer},
                device_id_type=mesh_ids,
            )

        def start(t, carry):
            copy_to(lax.rem(me + t, peers), me).start()
            return carry

        lax.fori_loop(1, peers, start, 0)
        dst[pl.ds(me, 1)] = src[pl.ds(me, 1)]
        cover()
        others = pl.ds(0, peers - 1)
        everyone = pltpu.make_async_remote_copy(
            src_ref=src.at[others],
            dst_ref=dst.at[others],
            send_sem=sends.at[phase],
            recv_sem=recvs.at[phase],
            device_id={"seq": lax.rem(me + 1, peers)},
            device_id_type=mesh_ids,
        )
        everyone.wait_send()
        everyone.wait_recv()

    def cat_cover():
        rows = lax.broadcasted_iota(jnp.int32, (cq.shape[0], cq.shape[0]), 0)
        cols = lax.broadcasted_iota(jnp.int32, (cq.shape[0], cq.shape[0]), 1)
        heads_inner(cq, ck, cv, cols <= rows, cat_inner)

    def resp_cover():
        heads_inner(rq, rk, rv, rmask[...] != 0, resp_inner)

    exchange(0, x_ref, got, cat_cover)

    def running(j, acc):
        payload[pl.ds(j, 1), pl.ds(0, half), :] = acc[None]
        return acc + got[j]

    total = lax.fori_loop(0, peers, running, jnp.zeros((half, DH), jnp.float32), unroll=8)

    def fill(j, carry):
        payload[pl.ds(j, 1), pl.ds(half, half), :] = total[None]
        return carry

    lax.fori_loop(0, peers, fill, 0, unroll=8)
    exchange(1, payload, back, resp_cover)

    partner = pltpu.make_async_remote_copy(
        src_ref=back.at[:, pl.ds(half, half)],
        dst_ref=whole.at[pl.ds(side * peers, peers)],
        send_sem=sends.at[2],
        recv_sem=recvs.at[2],
        device_id={"resp": 1 - side},
        device_id_type=mesh_ids,
    )
    partner.start()
    whole[pl.ds(side * peers, peers)] = back[:, pl.ds(half, half)]

    def prefix_of(h):
        return head_state(back, h, 0, half)

    heads_finish(cq, cat_inner, prefix_of, gain_ref, side * cq.shape[1], cat_out)
    partner.wait_send()
    arrived = pltpu.make_async_remote_copy(
        src_ref=back.at[:, pl.ds(half, half)],
        dst_ref=whole.at[pl.ds((1 - side) * peers, peers)],
        send_sem=sends.at[2],
        recv_sem=recvs.at[2],
        device_id={"resp": 1 - side},
        device_id_type=mesh_ids,
    )
    arrived.wait_recv()

    def total_of(h):
        return head_state(whole, h, 0, half)

    heads_finish(rq, resp_inner, total_of, gain_ref, 0, resp_out)


def layer(local_state, cat, resp, rmask, gain):
    peers = lax.axis_size("seq")
    chunks = local_state.reshape(peers, -1, DH)
    half = chunks.shape[1]
    vmem = pl.BlockSpec(memory_space=pltpu.VMEM)
    cat_rows, cat_width = cat[0].shape
    resp_rows, resp_width = resp[0].shape
    return pl.pallas_call(
        layer_kernel,
        out_shape=(
            jax.ShapeDtypeStruct(cat[0].shape, jnp.bfloat16),
            jax.ShapeDtypeStruct(resp[0].shape, jnp.bfloat16),
        ),
        in_specs=[vmem] * 9,
        out_specs=(vmem, vmem),
        scratch_shapes=[
            pltpu.VMEM((peers, half, DH), jnp.float32),
            pltpu.VMEM((peers, 2 * half, DH), jnp.float32),
            pltpu.VMEM((peers, 2 * half, DH), jnp.float32),
            pltpu.VMEM((2 * peers, half, DH), jnp.float32),
            pltpu.VMEM(cat[0].shape, jnp.float32),
            pltpu.VMEM(resp[0].shape, jnp.float32),
            pltpu.SemaphoreType.DMA((3,)),
            pltpu.SemaphoreType.DMA((3,)),
        ],
        compiler_params=pltpu.CompilerParams(has_side_effects=True),
        cost_estimate=pl.CostEstimate(
            flops=10 * DH * (cat_rows * cat_width + resp_rows * resp_width),
            transcendentals=cat_rows * cat_width // DH + resp_rows * resp_width // DH,
            bytes_accessed=14 * peers * half * DH,
        ),
    )(chunks, *cat, *resp, rmask, gain)


def per_device(
    cat_query, cat_key, cat_value, resp_query, resp_key, resp_value, resp_lengths, norm_gain
):
    heads_here = cat_query.shape[1] // DH
    local_state = block_state(cat_key, cat_value, heads_here)
    rows = jnp.arange(resp_query.shape[0], dtype=jnp.int32)
    ends = jnp.cumsum(resp_lengths[0])
    segment = jnp.sum((rows[:, None] >= ends[None, :]).astype(jnp.int32), axis=1)
    mask = (segment[:, None] == segment[None, :]) & (rows[None, :] <= rows[:, None])
    return layer(
        local_state,
        (cat_query, cat_key, cat_value),
        (resp_query, resp_key, resp_value),
        mask.astype(jnp.int32),
        norm_gain.reshape(1, -1),
    )


def solution(mesh):
    placed = (
        P("seq", "resp"),
        P("seq", "resp"),
        P("seq", "resp"),
        P(("seq", "resp"), None),
        P(("seq", "resp"), None),
        P(("seq", "resp"), None),
        P(("seq", "resp"), None),
        P(),
    )
    return jax.shard_map(
        per_device,
        mesh=mesh,
        in_specs=placed,
        out_specs=(P("seq", "resp"), P(("seq", "resp"), None)),
        check_vma=False,
    )
```

```python
import jax
import jax.numpy as jnp
from jax import lax
from jax.experimental import pallas as pl
from jax.experimental.pallas import tpu as pltpu
from jax.sharding import PartitionSpec as P

DH = 128
UNROLL = 4


def block_state(key, value, heads):
    rows = key.shape[0]
    kh = key.reshape(rows, heads, DH)
    vh = value.reshape(rows, heads, DH)
    return jnp.einsum("shd,she->hde", kh, vh, preferred_element_type=jnp.float32)


def heads_inner(q_ref, k_ref, v_ref, keep, o_ref):
    def one(h, carry):
        cols = pl.ds(pl.multiple_of(h * DH, DH), DH)
        scores = lax.dot_general(
            q_ref[:, cols], k_ref[:, cols], (((1,), (1,)), ((), ())),
            preferred_element_type=jnp.float32,
        )
        scores = jnp.where(keep, scores, 0.0).astype(jnp.bfloat16)
        o_ref[:, cols] = jnp.dot(scores, v_ref[:, cols], preferred_element_type=jnp.float32)
        return carry

    lax.fori_loop(0, q_ref.shape[1] // DH, one, 0, unroll=UNROLL)


def split_dot(q, state):
    hi = state.astype(jnp.bfloat16)
    rest = state - hi.astype(jnp.float32)
    mid = rest.astype(jnp.bfloat16)
    lo = (rest - mid.astype(jnp.float32)).astype(jnp.bfloat16)
    acc = jnp.dot(q, hi, preferred_element_type=jnp.float32)
    acc = acc + jnp.dot(q, mid, preferred_element_type=jnp.float32)
    return acc + jnp.dot(q, lo, preferred_element_type=jnp.float32)


def head_state(ref, h, first, half):
    if half <= DH:
        group = DH // half
        return ref[pl.ds(h * group, group), pl.ds(first, half), :].reshape(DH, DH)
    per = half // DH
    return ref[h // per, pl.ds(first + (h % per) * DH, DH), :]


def heads_finish(q_ref, inner_ref, state_of, gain_ref, gain_at, first, count, o_ref):
    def one(i, carry):
        cols = pl.ds(pl.multiple_of((first + i) * DH, DH), DH)
        raw = inner_ref[:, cols] + split_dot(q_ref[:, cols], state_of(i))
        square = jnp.mean(raw * raw, axis=-1, keepdims=True)
        gain = gain_ref[:, pl.ds(pl.multiple_of(gain_at + (first + i) * DH, DH), DH)]
        o_ref[:, cols] = (raw * lax.rsqrt(square + 1e-06) * gain).astype(o_ref.dtype)
        return carry

    lax.fori_loop(0, count, one, 0, unroll=UNROLL)


def layer_kernel(
    x_ref, cq, ck, cv, rq, rk, rv, rmask, gain_ref,
    cat_out, resp_out,
    got, payload, total_ref, before, totals, partner_totals, cat_inner, resp_inner, sends, recvs,
):
    peers, half = x_ref.shape[0], x_ref.shape[1]
    heads_here = cq.shape[1] // DH
    me = lax.axis_index("seq")
    side = lax.axis_index("resp")
    mesh_ids = pl.DeviceIdType.MESH

    def start_all(phase, src_of, dst):
        def start(t, carry):
            peer = lax.rem(me + t, peers)
            pltpu.make_async_remote_copy(
                src_ref=src_of(peer),
                dst_ref=dst.at[me],
                send_sem=sends.at[phase],
                recv_sem=recvs.at[phase],
                device_id={"seq": peer},
                device_id_type=mesh_ids,
            ).start()
            return carry

        lax.fori_loop(1, peers, start, 0)

    def wait_all(phase, dst):
        others = pl.ds(0, peers - 1)
        everyone = pltpu.make_async_remote_copy(
            src_ref=dst.at[others],
            dst_ref=dst.at[others],
            send_sem=sends.at[phase],
            recv_sem=recvs.at[phase],
            device_id={"seq": lax.rem(me + 1, peers)},
            device_id_type=mesh_ids,
        )
        everyone.wait_send()
        everyone.wait_recv()

    start_all(0, lambda peer: x_ref.at[peer], got)
    got[pl.ds(me, 1)] = x_ref[pl.ds(me, 1)]
    rows = lax.broadcasted_iota(jnp.int32, (cq.shape[0], cq.shape[0]), 0)
    cols = lax.broadcasted_iota(jnp.int32, (cq.shape[0], cq.shape[0]), 1)
    heads_inner(cq, ck, cv, cols <= rows, cat_inner)
    wait_all(0, got)

    def running(j, acc):
        payload[pl.ds(j, 1)] = acc[None]
        return acc + got[j]

    total_ref[...] = lax.fori_loop(
        0, peers, running, jnp.zeros((half, DH), jnp.float32), unroll=8
    )[None]
    start_all(1, lambda peer: payload.at[peer], before)
    start_all(2, lambda peer: total_ref.at[0], totals)
    before[pl.ds(me, 1)] = payload[pl.ds(me, 1)]
    totals[pl.ds(me, 1)] = total_ref[...]
    heads_inner(rq, rk, rv, rmask[...] != 0, resp_inner)

    wait_all(1, before)
    heads_finish(
        cq, cat_inner, lambda i: head_state(before, i, 0, half), gain_ref,
        side * cq.shape[1], 0, heads_here, cat_out,
    )
    wait_all(2, totals)
    partner = pltpu.make_async_remote_copy(
        src_ref=totals,
        dst_ref=partner_totals,
        send_sem=sends.at[3],
        recv_sem=recvs.at[3],
        device_id={"resp": 1 - side},
        device_id_type=mesh_ids,
    )
    partner.start()
    heads_finish(
        rq, resp_inner, lambda i: head_state(totals, i, 0, half), gain_ref,
        0, side * heads_here, heads_here, resp_out,
    )
    partner.wait_send()
    partner.wait_recv()
    heads_finish(
        rq, resp_inner, lambda i: head_state(partner_totals, i, 0, half), gain_ref,
        0, (1 - side) * heads_here, heads_here, resp_out,
    )


def layer(local_state, cat, resp, rmask, gain):
    peers = lax.axis_size("seq")
    chunks = local_state.reshape(peers, -1, DH)
    half = chunks.shape[1]
    vmem = pl.BlockSpec(memory_space=pltpu.VMEM)
    cat_rows, cat_width = cat[0].shape
    resp_rows, resp_width = resp[0].shape
    return pl.pallas_call(
        layer_kernel,
        out_shape=(
            jax.ShapeDtypeStruct(cat[0].shape, jnp.bfloat16),
            jax.ShapeDtypeStruct(resp[0].shape, jnp.bfloat16),
        ),
        in_specs=[vmem] * 9,
        out_specs=(vmem, vmem),
        scratch_shapes=[
            pltpu.VMEM((peers, half, DH), jnp.float32),
            pltpu.VMEM((peers, half, DH), jnp.float32),
            pltpu.VMEM((1, half, DH), jnp.float32),
            pltpu.VMEM((peers, half, DH), jnp.float32),
            pltpu.VMEM((peers, half, DH), jnp.float32),
            pltpu.VMEM((peers, half, DH), jnp.float32),
            pltpu.VMEM(cat[0].shape, jnp.float32),
            pltpu.VMEM(resp[0].shape, jnp.float32),
            pltpu.SemaphoreType.DMA((4,)),
            pltpu.SemaphoreType.DMA((4,)),
        ],
        compiler_params=pltpu.CompilerParams(has_side_effects=True),
        cost_estimate=pl.CostEstimate(
            flops=10 * DH * (cat_rows * cat_width + resp_rows * resp_width),
            transcendentals=cat_rows * cat_width // DH + resp_rows * resp_width // DH,
            bytes_accessed=14 * peers * half * DH,
        ),
    )(chunks, *cat, *resp, rmask, gain)


def per_device(
    cat_query, cat_key, cat_value, resp_query, resp_key, resp_value, resp_lengths, norm_gain
):
    heads_here = cat_query.shape[1] // DH
    local_state = block_state(cat_key, cat_value, heads_here)
    rows = jnp.arange(resp_query.shape[0], dtype=jnp.int32)
    ends = jnp.cumsum(resp_lengths[0])
    segment = jnp.sum((rows[:, None] >= ends[None, :]).astype(jnp.int32), axis=1)
    mask = (segment[:, None] == segment[None, :]) & (rows[None, :] <= rows[:, None])
    return layer(
        local_state,
        (cat_query, cat_key, cat_value),
        (resp_query, resp_key, resp_value),
        mask.astype(jnp.int32),
        norm_gain.reshape(1, -1),
    )


def solution(mesh):
    placed = (
        P("seq", "resp"),
        P("seq", "resp"),
        P("seq", "resp"),
        P(("seq", "resp"), None),
        P(("seq", "resp"), None),
        P(("seq", "resp"), None),
        P(("seq", "resp"), None),
        P(),
    )
    return jax.shard_map(
        per_device,
        mesh=mesh,
        in_specs=placed,
        out_specs=(P("seq", "resp"), P(("seq", "resp"), None)),
        check_vma=False,
    )
```

```python
import jax
import jax.numpy as jnp
from jax import lax
from jax.experimental import pallas as pl
from jax.experimental.pallas import tpu as pltpu
from jax.sharding import PartitionSpec as P

DH = 128
UNROLL = 8


def block_state(key, value, heads):
    rows = key.shape[0]
    kh = key.reshape(rows, heads, DH)
    vh = value.reshape(rows, heads, DH)
    return jnp.einsum("shd,she->hde", kh, vh, preferred_element_type=jnp.float32)


def heads_inner(q_ref, k_ref, v_ref, keep, o_ref):
    def one(h, carry):
        cols = pl.ds(pl.multiple_of(h * DH, DH), DH)
        scores = lax.dot_general(
            q_ref[:, cols], k_ref[:, cols], (((1,), (1,)), ((), ())),
            preferred_element_type=jnp.float32,
        )
        scores = jnp.where(keep, scores, 0.0).astype(jnp.bfloat16)
        o_ref[:, cols] = jnp.dot(scores, v_ref[:, cols], preferred_element_type=jnp.float32)
        return carry

    lax.fori_loop(0, q_ref.shape[1] // DH, one, 0, unroll=UNROLL)


def split_dot(q, state):
    hi = state.astype(jnp.bfloat16)
    rest = state - hi.astype(jnp.float32)
    mid = rest.astype(jnp.bfloat16)
    lo = (rest - mid.astype(jnp.float32)).astype(jnp.bfloat16)
    acc = jnp.dot(q, hi, preferred_element_type=jnp.float32)
    acc = acc + jnp.dot(q, mid, preferred_element_type=jnp.float32)
    return acc + jnp.dot(q, lo, preferred_element_type=jnp.float32)


def head_state(ref, h, first, half):
    if half <= DH:
        group = DH // half
        return ref[pl.ds(h * group, group), pl.ds(first, half), :].reshape(DH, DH)
    per = half // DH
    return ref[h // per, pl.ds(first + (h % per) * DH, DH), :]


def put_head_state(ref, h, value, half):
    if half <= DH:
        group = DH // half
        ref[pl.ds(h * group, group)] = value.reshape(group, half, DH)
    else:
        per = half // DH
        ref[h // per, pl.ds((h % per) * DH, DH), :] = value


def heads_finish(q_ref, inner_ref, state_of, gain_ref, gain_at, first, count, o_ref):
    def one(i, carry):
        cols = pl.ds(pl.multiple_of((first + i) * DH, DH), DH)
        raw = inner_ref[:, cols] + split_dot(q_ref[:, cols], state_of(i))
        square = jnp.mean(raw * raw, axis=-1, keepdims=True)
        gain = gain_ref[:, pl.ds(pl.multiple_of(gain_at + (first + i) * DH, DH), DH)]
        o_ref[:, cols] = (raw * lax.rsqrt(square + 1e-06) * gain).astype(o_ref.dtype)
        return carry

    lax.fori_loop(0, count, one, 0, unroll=UNROLL)


def layer_kernel(
    cq, ck, cv, rq, rk, rv, lengths, gain_ref,
    cat_out, resp_out,
    x_ref, got, payload, total_ref, before, totals, partner_totals, cat_inner, resp_inner,
    sends, recvs,
):
    peers, half = x_ref.shape[0], x_ref.shape[1]
    heads_here = cq.shape[1] // DH

    def own_state(h, carry):
        cols = pl.ds(pl.multiple_of(h * DH, DH), DH)
        value = lax.dot_general(
            ck[:, cols], cv[:, cols], (((0,), (0,)), ((), ())),
            preferred_element_type=jnp.float32,
        )
        put_head_state(x_ref, h, value, half)
        return carry

    lax.fori_loop(0, heads_here, own_state, 0, unroll=UNROLL)
    me = lax.axis_index("seq")
    side = lax.axis_index("resp")
    mesh_ids = pl.DeviceIdType.MESH

    def start_all(phase, src_of, dst):
        def start(t, carry):
            peer = lax.rem(me + t, peers)
            pltpu.make_async_remote_copy(
                src_ref=src_of(peer),
                dst_ref=dst.at[me],
                send_sem=sends.at[phase],
                recv_sem=recvs.at[phase],
                device_id={"seq": peer},
                device_id_type=mesh_ids,
            ).start()
            return carry

        lax.fori_loop(1, peers, start, 0)

    def wait_all(phase, dst):
        others = pl.ds(0, peers - 1)
        everyone = pltpu.make_async_remote_copy(
            src_ref=dst.at[others],
            dst_ref=dst.at[others],
            send_sem=sends.at[phase],
            recv_sem=recvs.at[phase],
            device_id={"seq": lax.rem(me + 1, peers)},
            device_id_type=mesh_ids,
        )
        everyone.wait_send()
        everyone.wait_recv()

    start_all(0, lambda peer: x_ref.at[peer], got)
    got[pl.ds(me, 1)] = x_ref[pl.ds(me, 1)]
    rows = lax.broadcasted_iota(jnp.int32, (cq.shape[0], cq.shape[0]), 0)
    cols = lax.broadcasted_iota(jnp.int32, (cq.shape[0], cq.shape[0]), 1)
    heads_inner(cq, ck, cv, cols <= rows, cat_inner)
    wait_all(0, got)

    def running(j, acc):
        payload[pl.ds(j, 1)] = acc[None]
        return acc + got[j]

    total_ref[...] = lax.fori_loop(
        0, peers, running, jnp.zeros((half, DH), jnp.float32), unroll=8
    )[None]
    start_all(1, lambda peer: payload.at[peer], before)
    start_all(2, lambda peer: total_ref.at[0], totals)
    before[pl.ds(me, 1)] = payload[pl.ds(me, 1)]
    totals[pl.ds(me, 1)] = total_ref[...]
    rrows = lax.broadcasted_iota(jnp.int32, (rq.shape[0], rq.shape[0]), 0)
    rcols = lax.broadcasted_iota(jnp.int32, (rq.shape[0], rq.shape[0]), 1)
    end = lengths[0, 0]
    row_seg = (rrows >= end).astype(jnp.int32)
    col_seg = (rcols >= end).astype(jnp.int32)
    for k in range(1, lengths.shape[1]):
        end = end + lengths[0, k]
        row_seg = row_seg + (rrows >= end).astype(jnp.int32)
        col_seg = col_seg + (rcols >= end).astype(jnp.int32)
    heads_inner(rq, rk, rv, (row_seg == col_seg) & (rcols <= rrows), resp_inner)

    wait_all(1, before)
    heads_finish(
        cq, cat_inner, lambda i: head_state(before, i, 0, half), gain_ref,
        side * cq.shape[1], 0, heads_here, cat_out,
    )
    wait_all(2, totals)
    partner = pltpu.make_async_remote_copy(
        src_ref=totals,
        dst_ref=partner_totals,
        send_sem=sends.at[3],
        recv_sem=recvs.at[3],
        device_id={"resp": 1 - side},
        device_id_type=mesh_ids,
    )
    partner.start()
    heads_finish(
        rq, resp_inner, lambda i: head_state(totals, i, 0, half), gain_ref,
        0, side * heads_here, heads_here, resp_out,
    )
    partner.wait_send()
    partner.wait_recv()
    heads_finish(
        rq, resp_inner, lambda i: head_state(partner_totals, i, 0, half), gain_ref,
        0, (1 - side) * heads_here, heads_here, resp_out,
    )


def layer(cat, resp, lengths, gain):
    peers = lax.axis_size("seq")
    half = cat[0].shape[1] // peers
    vmem = pl.BlockSpec(memory_space=pltpu.VMEM)
    cat_rows, cat_width = cat[0].shape
    resp_rows, resp_width = resp[0].shape
    return pl.pallas_call(
        layer_kernel,
        out_shape=(
            jax.ShapeDtypeStruct(cat[0].shape, jnp.bfloat16),
            jax.ShapeDtypeStruct(resp[0].shape, jnp.bfloat16),
        ),
        in_specs=[vmem] * 6 + [pl.BlockSpec(memory_space=pltpu.SMEM), vmem],
        out_specs=(vmem, vmem),
        scratch_shapes=[
            pltpu.VMEM((peers, half, DH), jnp.float32),
            pltpu.VMEM((peers, half, DH), jnp.float32),
            pltpu.VMEM((peers, half, DH), jnp.float32),
            pltpu.VMEM((1, half, DH), jnp.float32),
            pltpu.VMEM((peers, half, DH), jnp.float32),
            pltpu.VMEM((peers, half, DH), jnp.float32),
            pltpu.VMEM((peers, half, DH), jnp.float32),
            pltpu.VMEM(cat[0].shape, jnp.float32),
            pltpu.VMEM(resp[0].shape, jnp.float32),
            pltpu.SemaphoreType.DMA((4,)),
            pltpu.SemaphoreType.DMA((4,)),
        ],
        compiler_params=pltpu.CompilerParams(has_side_effects=True),
        cost_estimate=pl.CostEstimate(
            flops=10 * DH * (cat_rows * cat_width + resp_rows * resp_width),
            transcendentals=cat_rows * cat_width // DH + resp_rows * resp_width // DH,
            bytes_accessed=14 * peers * half * DH,
        ),
    )(*cat, *resp, lengths, gain)


def per_device(
    cat_query, cat_key, cat_value, resp_query, resp_key, resp_value, resp_lengths, norm_gain
):
    return layer(
        (cat_query, cat_key, cat_value),
        (resp_query, resp_key, resp_value),
        resp_lengths,
        norm_gain.reshape(1, -1),
    )


def solution(mesh):
    placed = (
        P("seq", "resp"),
        P("seq", "resp"),
        P("seq", "resp"),
        P(("seq", "resp"), None),
        P(("seq", "resp"), None),
        P(("seq", "resp"), None),
        P(("seq", "resp"), None),
        P(),
    )
    return jax.shard_map(
        per_device,
        mesh=mesh,
        in_specs=placed,
        out_specs=(P("seq", "resp"), P(("seq", "resp"), None)),
        check_vma=False,
    )
```

```python
import jax
import jax.numpy as jnp
from jax import lax
from jax.experimental import pallas as pl
from jax.experimental.pallas import tpu as pltpu
from jax.sharding import PartitionSpec as P

DH = 128
UNROLL = 8


def block_state(key, value, heads):
    rows = key.shape[0]
    kh = key.reshape(rows, heads, DH)
    vh = value.reshape(rows, heads, DH)
    return jnp.einsum("shd,she->hde", kh, vh, preferred_element_type=jnp.float32)


def heads_inner(q_ref, k_ref, v_ref, keep, o_ref):
    def one(h, carry):
        cols = pl.ds(pl.multiple_of(h * DH, DH), DH)
        scores = lax.dot_general(
            q_ref[:, cols], k_ref[:, cols], (((1,), (1,)), ((), ())),
            preferred_element_type=jnp.float32,
        )
        scores = jnp.where(keep, scores, 0.0).astype(jnp.bfloat16)
        o_ref[:, cols] = jnp.dot(scores, v_ref[:, cols], preferred_element_type=jnp.float32)
        return carry

    lax.fori_loop(0, q_ref.shape[1] // DH, one, 0, unroll=UNROLL)


def split_dot(q, state):
    hi = state.astype(jnp.bfloat16)
    rest = state - hi.astype(jnp.float32)
    mid = rest.astype(jnp.bfloat16)
    lo = (rest - mid.astype(jnp.float32)).astype(jnp.bfloat16)
    acc = jnp.dot(q, hi, preferred_element_type=jnp.float32)
    acc = acc + jnp.dot(q, mid, preferred_element_type=jnp.float32)
    return acc + jnp.dot(q, lo, preferred_element_type=jnp.float32)


def head_state(ref, h, first, half):
    if half <= DH:
        group = DH // half
        return ref[pl.ds(h * group, group), pl.ds(first, half), :].reshape(DH, DH)
    per = half // DH
    return ref[h // per, pl.ds(first + (h % per) * DH, DH), :]


def put_head_state(ref, h, value, half):
    if half <= DH:
        group = DH // half
        ref[pl.ds(h * group, group)] = value.reshape(group, half, DH)
    else:
        per = half // DH
        ref[h // per, pl.ds((h % per) * DH, DH), :] = value


def heads_finish(q_ref, inner_ref, state_of, gain_ref, gain_at, first, count, o_ref):
    def one(i, carry):
        cols = pl.ds(pl.multiple_of((first + i) * DH, DH), DH)
        raw = inner_ref[:, cols] + split_dot(q_ref[:, cols], state_of(i))
        square = jnp.mean(raw * raw, axis=-1, keepdims=True)
        gain = gain_ref[:, pl.ds(pl.multiple_of(gain_at + (first + i) * DH, DH), DH)]
        o_ref[:, cols] = (raw * lax.rsqrt(square + 1e-06) * gain).astype(o_ref.dtype)
        return carry

    lax.fori_loop(0, count, one, 0, unroll=UNROLL)


def layer_kernel(
    cq, ck, cv, rq, rk, rv, lengths, gain_ref,
    cat_out, resp_out,
    x_ref, got, payload, total_ref, before, totals, partner_totals, cat_inner, resp_inner,
    sends, recvs,
):
    peers, half = x_ref.shape[0], x_ref.shape[1]
    heads_here = cq.shape[1] // DH
    me = lax.axis_index("seq")
    side = lax.axis_index("resp")
    mesh_ids = pl.DeviceIdType.MESH
    barrier = pltpu.get_barrier_semaphore()

    def greet(t, carry):
        pl.semaphore_signal(
            barrier, 1, device_id={"seq": lax.rem(me + t, peers)}, device_id_type=mesh_ids
        )
        return carry

    lax.fori_loop(1, peers, greet, 0)
    pl.semaphore_signal(barrier, 1, device_id={"resp": 1 - side}, device_id_type=mesh_ids)

    def own_state(h, carry):
        cols = pl.ds(pl.multiple_of(h * DH, DH), DH)
        value = lax.dot_general(
            ck[:, cols], cv[:, cols], (((0,), (0,)), ((), ())),
            preferred_element_type=jnp.float32,
        )
        put_head_state(x_ref, h, value, half)
        return carry

    lax.fori_loop(0, heads_here, own_state, 0, unroll=UNROLL)
    pl.semaphore_wait(barrier, peers)

    def start_all(phase, src_of, dst):
        def start(t, carry):
            peer = lax.rem(me + t, peers)
            pltpu.make_async_remote_copy(
                src_ref=src_of(peer),
                dst_ref=dst.at[me],
                send_sem=sends.at[phase],
                recv_sem=recvs.at[phase],
                device_id={"seq": peer},
                device_id_type=mesh_ids,
            ).start()
            return carry

        lax.fori_loop(1, peers, start, 0)

    def wait_all(phase, dst):
        others = pl.ds(0, peers - 1)
        everyone = pltpu.make_async_remote_copy(
            src_ref=dst.at[others],
            dst_ref=dst.at[others],
            send_sem=sends.at[phase],
            recv_sem=recvs.at[phase],
            device_id={"seq": lax.rem(me + 1, peers)},
            device_id_type=mesh_ids,
        )
        everyone.wait_send()
        everyone.wait_recv()

    start_all(0, lambda peer: x_ref.at[peer], got)
    got[pl.ds(me, 1)] = x_ref[pl.ds(me, 1)]
    rows = lax.broadcasted_iota(jnp.int32, (cq.shape[0], cq.shape[0]), 0)
    cols = lax.broadcasted_iota(jnp.int32, (cq.shape[0], cq.shape[0]), 1)
    heads_inner(cq, ck, cv, cols <= rows, cat_inner)
    wait_all(0, got)

    def running(j, acc):
        payload[pl.ds(j, 1)] = acc[None]
        return acc + got[j]

    total_ref[...] = lax.fori_loop(
        0, peers, running, jnp.zeros((half, DH), jnp.float32), unroll=8
    )[None]
    start_all(1, lambda peer: payload.at[peer], before)
    start_all(2, lambda peer: total_ref.at[0], totals)
    before[pl.ds(me, 1)] = payload[pl.ds(me, 1)]
    totals[pl.ds(me, 1)] = total_ref[...]
    rrows = lax.broadcasted_iota(jnp.int32, (rq.shape[0], rq.shape[0]), 0)
    rcols = lax.broadcasted_iota(jnp.int32, (rq.shape[0], rq.shape[0]), 1)
    end = lengths[0, 0]
    row_seg = (rrows >= end).astype(jnp.int32)
    col_seg = (rcols >= end).astype(jnp.int32)
    for k in range(1, lengths.shape[1]):
        end = end + lengths[0, k]
        row_seg = row_seg + (rrows >= end).astype(jnp.int32)
        col_seg = col_seg + (rcols >= end).astype(jnp.int32)
    heads_inner(rq, rk, rv, (row_seg == col_seg) & (rcols <= rrows), resp_inner)

    wait_all(1, before)
    heads_finish(
        cq, cat_inner, lambda i: head_state(before, i, 0, half), gain_ref,
        side * cq.shape[1], 0, heads_here, cat_out,
    )
    wait_all(2, totals)
    partner = pltpu.make_async_remote_copy(
        src_ref=totals,
        dst_ref=partner_totals,
        send_sem=sends.at[3],
        recv_sem=recvs.at[3],
        device_id={"resp": 1 - side},
        device_id_type=mesh_ids,
    )
    partner.start()
    heads_finish(
        rq, resp_inner, lambda i: head_state(totals, i, 0, half), gain_ref,
        0, side * heads_here, heads_here, resp_out,
    )
    partner.wait_send()
    partner.wait_recv()
    heads_finish(
        rq, resp_inner, lambda i: head_state(partner_totals, i, 0, half), gain_ref,
        0, (1 - side) * heads_here, heads_here, resp_out,
    )


def layer(cat, resp, lengths, gain):
    peers = lax.axis_size("seq")
    half = cat[0].shape[1] // peers
    vmem = pl.BlockSpec(memory_space=pltpu.VMEM)
    cat_rows, cat_width = cat[0].shape
    resp_rows, resp_width = resp[0].shape
    return pl.pallas_call(
        layer_kernel,
        out_shape=(
            jax.ShapeDtypeStruct(cat[0].shape, jnp.bfloat16),
            jax.ShapeDtypeStruct(resp[0].shape, jnp.bfloat16),
        ),
        in_specs=[vmem] * 6 + [pl.BlockSpec(memory_space=pltpu.SMEM), vmem],
        out_specs=(vmem, vmem),
        scratch_shapes=[
            pltpu.VMEM((peers, half, DH), jnp.float32),
            pltpu.VMEM((peers, half, DH), jnp.float32),
            pltpu.VMEM((peers, half, DH), jnp.float32),
            pltpu.VMEM((1, half, DH), jnp.float32),
            pltpu.VMEM((peers, half, DH), jnp.float32),
            pltpu.VMEM((peers, half, DH), jnp.float32),
            pltpu.VMEM((peers, half, DH), jnp.float32),
            pltpu.VMEM(cat[0].shape, jnp.float32),
            pltpu.VMEM(resp[0].shape, jnp.float32),
            pltpu.SemaphoreType.DMA((4,)),
            pltpu.SemaphoreType.DMA((4,)),
        ],
        compiler_params=pltpu.CompilerParams(collective_id=0, has_side_effects=True),
        cost_estimate=pl.CostEstimate(
            flops=10 * DH * (cat_rows * cat_width + resp_rows * resp_width),
            transcendentals=cat_rows * cat_width // DH + resp_rows * resp_width // DH,
            bytes_accessed=14 * peers * half * DH,
        ),
    )(*cat, *resp, lengths, gain)


def per_device(
    cat_query, cat_key, cat_value, resp_query, resp_key, resp_value, resp_lengths, norm_gain
):
    return layer(
        (cat_query, cat_key, cat_value),
        (resp_query, resp_key, resp_value),
        resp_lengths,
        norm_gain.reshape(1, -1),
    )


def solution(mesh):
    placed = (
        P("seq", "resp"),
        P("seq", "resp"),
        P("seq", "resp"),
        P(("seq", "resp"), None),
        P(("seq", "resp"), None),
        P(("seq", "resp"), None),
        P(("seq", "resp"), None),
        P(),
    )
    return jax.shard_map(
        per_device,
        mesh=mesh,
        in_specs=placed,
        out_specs=(P("seq", "resp"), P(("seq", "resp"), None)),
        check_vma=False,
    )
```

```python
import jax
import jax.numpy as jnp
from jax import lax
from jax.experimental import pallas as pl
from jax.experimental.pallas import tpu as pltpu
from jax.sharding import PartitionSpec as P

DH = 128
UNROLL = 8


def block_state(key, value, heads):
    rows = key.shape[0]
    kh = key.reshape(rows, heads, DH)
    vh = value.reshape(rows, heads, DH)
    return jnp.einsum("shd,she->hde", kh, vh, preferred_element_type=jnp.float32)


def heads_inner(q_ref, k_ref, v_ref, keep, o_ref):
    def one(h, carry):
        cols = pl.ds(pl.multiple_of(h * DH, DH), DH)
        scores = lax.dot_general(
            q_ref[:, cols], k_ref[:, cols], (((1,), (1,)), ((), ())),
            preferred_element_type=jnp.float32,
        )
        scores = jnp.where(keep, scores, 0.0).astype(jnp.bfloat16)
        o_ref[:, cols] = jnp.dot(scores, v_ref[:, cols], preferred_element_type=jnp.float32)
        return carry

    lax.fori_loop(0, q_ref.shape[1] // DH, one, 0, unroll=UNROLL)


def split_dot(q, state):
    hi = state.astype(jnp.bfloat16)
    rest = state - hi.astype(jnp.float32)
    mid = rest.astype(jnp.bfloat16)
    lo = (rest - mid.astype(jnp.float32)).astype(jnp.bfloat16)
    acc = jnp.dot(q, hi, preferred_element_type=jnp.float32)
    acc = acc + jnp.dot(q, mid, preferred_element_type=jnp.float32)
    return acc + jnp.dot(q, lo, preferred_element_type=jnp.float32)


def head_state(ref, h, first, half):
    if half <= DH:
        group = DH // half
        return ref[pl.ds(h * group, group), pl.ds(first, half), :].reshape(DH, DH)
    per = half // DH
    return ref[h // per, pl.ds(first + (h % per) * DH, DH), :]


def put_head_state(ref, h, value, half):
    if half <= DH:
        group = DH // half
        ref[pl.ds(h * group, group)] = value.reshape(group, half, DH)
    else:
        per = half // DH
        ref[h // per, pl.ds((h % per) * DH, DH), :] = value


def heads_finish(q_ref, inner_ref, state_of, gain_ref, gain_at, first, count, o_ref):
    def one(i, carry):
        cols = pl.ds(pl.multiple_of((first + i) * DH, DH), DH)
        raw = inner_ref[:, cols] + split_dot(q_ref[:, cols], state_of(i))
        square = jnp.mean(raw * raw, axis=-1, keepdims=True)
        gain = gain_ref[:, pl.ds(pl.multiple_of(gain_at + (first + i) * DH, DH), DH)]
        o_ref[:, cols] = (raw * lax.rsqrt(square + 1e-06) * gain).astype(o_ref.dtype)
        return carry

    lax.fori_loop(0, count, one, 0, unroll=UNROLL)


def layer_kernel(
    cq, ck, cv, rq, rk, rv, lengths, gain_ref,
    cat_out, resp_out,
    x_ref, got, payload, total_ref, before, totals, partner_totals, cat_inner, resp_inner,
    sends, recvs,
):
    peers, half = x_ref.shape[0], x_ref.shape[1]
    heads_here = cq.shape[1] // DH
    me = lax.axis_index("seq")
    side = lax.axis_index("resp")
    mesh_ids = pl.DeviceIdType.MESH
    barrier = pltpu.get_barrier_semaphore()

    def greet(t, carry):
        pl.semaphore_signal(
            barrier, 1, device_id={"seq": lax.rem(me + t, peers)}, device_id_type=mesh_ids
        )
        return carry

    lax.fori_loop(1, peers, greet, 0)
    pl.semaphore_signal(barrier, 1, device_id={"resp": 1 - side}, device_id_type=mesh_ids)

    def own_state(h, carry):
        cols = pl.ds(pl.multiple_of(h * DH, DH), DH)
        value = lax.dot_general(
            ck[:, cols], cv[:, cols], (((0,), (0,)), ((), ())),
            preferred_element_type=jnp.float32,
        )
        put_head_state(x_ref, h, value, half)
        return carry

    lax.fori_loop(0, heads_here, own_state, 0, unroll=UNROLL)
    pl.semaphore_wait(barrier, peers)

    part = half // 2

    def start_all(phase, src_of, dst, k):
        def start(t, carry):
            peer = lax.rem(me + t, peers)
            pltpu.make_async_remote_copy(
                src_ref=src_of(peer),
                dst_ref=dst.at[me, pl.ds(k * part, part)],
                send_sem=sends.at[phase],
                recv_sem=recvs.at[phase],
                device_id={"seq": peer},
                device_id_type=mesh_ids,
            ).start()
            return carry

        lax.fori_loop(1, peers, start, 0)

    def wait_all(phase, dst, k):
        others = pl.ds(0, peers - 1)
        everyone = pltpu.make_async_remote_copy(
            src_ref=dst.at[others, pl.ds(k * part, part)],
            dst_ref=dst.at[others, pl.ds(k * part, part)],
            send_sem=sends.at[phase],
            recv_sem=recvs.at[phase],
            device_id={"seq": lax.rem(me + 1, peers)},
            device_id_type=mesh_ids,
        )
        everyone.wait_send()
        everyone.wait_recv()

    for k in range(2):
        start_all(k, lambda peer, k=k: x_ref.at[peer, pl.ds(k * part, part)], got, k)
    got[pl.ds(me, 1)] = x_ref[pl.ds(me, 1)]
    rows = lax.broadcasted_iota(jnp.int32, (cq.shape[0], cq.shape[0]), 0)
    cols = lax.broadcasted_iota(jnp.int32, (cq.shape[0], cq.shape[0]), 1)
    heads_inner(cq, ck, cv, cols <= rows, cat_inner)

    for k in range(2):
        wait_all(k, got, k)
        rows_k = pl.ds(k * part, part)

        def running(j, acc, rows_k=rows_k):
            payload[pl.ds(j, 1), rows_k] = acc[None]
            return acc + got[j, rows_k]

        total_ref[:, rows_k] = lax.fori_loop(
            0, peers, running, jnp.zeros((part, DH), jnp.float32), unroll=8
        )[None]
        start_all(2 + k, lambda peer, rows_k=rows_k: payload.at[peer, rows_k], before, k)
        start_all(4 + k, lambda peer, rows_k=rows_k: total_ref.at[0, rows_k], totals, k)
    before[pl.ds(me, 1)] = payload[pl.ds(me, 1)]
    totals[pl.ds(me, 1)] = total_ref[...]
    rrows = lax.broadcasted_iota(jnp.int32, (rq.shape[0], rq.shape[0]), 0)
    rcols = lax.broadcasted_iota(jnp.int32, (rq.shape[0], rq.shape[0]), 1)
    end = lengths[0, 0]
    row_seg = (rrows >= end).astype(jnp.int32)
    col_seg = (rcols >= end).astype(jnp.int32)
    for k in range(1, lengths.shape[1]):
        end = end + lengths[0, k]
        row_seg = row_seg + (rrows >= end).astype(jnp.int32)
        col_seg = col_seg + (rcols >= end).astype(jnp.int32)
    heads_inner(rq, rk, rv, (row_seg == col_seg) & (rcols <= rrows), resp_inner)

    wait_all(2, before, 0)
    wait_all(3, before, 1)
    heads_finish(
        cq, cat_inner, lambda i: head_state(before, i, 0, half), gain_ref,
        side * cq.shape[1], 0, heads_here, cat_out,
    )
    wait_all(4, totals, 0)
    wait_all(5, totals, 1)
    partner = pltpu.make_async_remote_copy(
        src_ref=totals,
        dst_ref=partner_totals,
        send_sem=sends.at[6],
        recv_sem=recvs.at[6],
        device_id={"resp": 1 - side},
        device_id_type=mesh_ids,
    )
    partner.start()
    heads_finish(
        rq, resp_inner, lambda i: head_state(totals, i, 0, half), gain_ref,
        0, side * heads_here, heads_here, resp_out,
    )
    partner.wait_send()
    partner.wait_recv()
    heads_finish(
        rq, resp_inner, lambda i: head_state(partner_totals, i, 0, half), gain_ref,
        0, (1 - side) * heads_here, heads_here, resp_out,
    )


def layer(cat, resp, lengths, gain):
    peers = lax.axis_size("seq")
    half = cat[0].shape[1] // peers
    vmem = pl.BlockSpec(memory_space=pltpu.VMEM)
    cat_rows, cat_width = cat[0].shape
    resp_rows, resp_width = resp[0].shape
    return pl.pallas_call(
        layer_kernel,
        out_shape=(
            jax.ShapeDtypeStruct(cat[0].shape, jnp.bfloat16),
            jax.ShapeDtypeStruct(resp[0].shape, jnp.bfloat16),
        ),
        in_specs=[vmem] * 6 + [pl.BlockSpec(memory_space=pltpu.SMEM), vmem],
        out_specs=(vmem, vmem),
        scratch_shapes=[
            pltpu.VMEM((peers, half, DH), jnp.float32),
            pltpu.VMEM((peers, half, DH), jnp.float32),
            pltpu.VMEM((peers, half, DH), jnp.float32),
            pltpu.VMEM((1, half, DH), jnp.float32),
            pltpu.VMEM((peers, half, DH), jnp.float32),
            pltpu.VMEM((peers, half, DH), jnp.float32),
            pltpu.VMEM((peers, half, DH), jnp.float32),
            pltpu.VMEM(cat[0].shape, jnp.float32),
            pltpu.VMEM(resp[0].shape, jnp.float32),
            pltpu.SemaphoreType.DMA((7,)),
            pltpu.SemaphoreType.DMA((7,)),
        ],
        compiler_params=pltpu.CompilerParams(collective_id=0, has_side_effects=True),
        cost_estimate=pl.CostEstimate(
            flops=10 * DH * (cat_rows * cat_width + resp_rows * resp_width),
            transcendentals=cat_rows * cat_width // DH + resp_rows * resp_width // DH,
            bytes_accessed=14 * peers * half * DH,
        ),
    )(*cat, *resp, lengths, gain)


def per_device(
    cat_query, cat_key, cat_value, resp_query, resp_key, resp_value, resp_lengths, norm_gain
):
    return layer(
        (cat_query, cat_key, cat_value),
        (resp_query, resp_key, resp_value),
        resp_lengths,
        norm_gain.reshape(1, -1),
    )


def solution(mesh):
    placed = (
        P("seq", "resp"),
        P("seq", "resp"),
        P("seq", "resp"),
        P(("seq", "resp"), None),
        P(("seq", "resp"), None),
        P(("seq", "resp"), None),
        P(("seq", "resp"), None),
        P(),
    )
    return jax.shard_map(
        per_device,
        mesh=mesh,
        in_specs=placed,
        out_specs=(P("seq", "resp"), P(("seq", "resp"), None)),
        check_vma=False,
    )
```

```python
import jax
import jax.numpy as jnp
from jax import lax
from jax.experimental import pallas as pl
from jax.experimental.pallas import tpu as pltpu
from jax.sharding import PartitionSpec as P

DH = 128
UNROLL = 8
PARTS = 4


def block_state(key, value, heads):
    rows = key.shape[0]
    kh = key.reshape(rows, heads, DH)
    vh = value.reshape(rows, heads, DH)
    return jnp.einsum("shd,she->hde", kh, vh, preferred_element_type=jnp.float32)


def heads_inner(q_ref, k_ref, v_ref, keep, o_ref):
    def one(h, carry):
        cols = pl.ds(pl.multiple_of(h * DH, DH), DH)
        scores = lax.dot_general(
            q_ref[:, cols], k_ref[:, cols], (((1,), (1,)), ((), ())),
            preferred_element_type=jnp.float32,
        )
        scores = jnp.where(keep, scores, 0.0).astype(jnp.bfloat16)
        o_ref[:, cols] = jnp.dot(scores, v_ref[:, cols], preferred_element_type=jnp.float32)
        return carry

    lax.fori_loop(0, q_ref.shape[1] // DH, one, 0, unroll=UNROLL)


def split_dot(q, state):
    hi = state.astype(jnp.bfloat16)
    rest = state - hi.astype(jnp.float32)
    mid = rest.astype(jnp.bfloat16)
    lo = (rest - mid.astype(jnp.float32)).astype(jnp.bfloat16)
    acc = jnp.dot(q, hi, preferred_element_type=jnp.float32)
    acc = acc + jnp.dot(q, mid, preferred_element_type=jnp.float32)
    return acc + jnp.dot(q, lo, preferred_element_type=jnp.float32)


def head_state(ref, h, first, half):
    if half <= DH:
        group = DH // half
        return ref[pl.ds(h * group, group), pl.ds(first, half), :].reshape(DH, DH)
    per = half // DH
    return ref[h // per, pl.ds(first + (h % per) * DH, DH), :]


def put_head_state(ref, h, value, half):
    if half <= DH:
        group = DH // half
        ref[pl.ds(h * group, group)] = value.reshape(group, half, DH)
    else:
        per = half // DH
        ref[h // per, pl.ds((h % per) * DH, DH), :] = value


def heads_finish(q_ref, inner_ref, state_of, gain_ref, gain_at, first, count, o_ref):
    def one(i, carry):
        cols = pl.ds(pl.multiple_of((first + i) * DH, DH), DH)
        raw = inner_ref[:, cols] + split_dot(q_ref[:, cols], state_of(i))
        square = jnp.mean(raw * raw, axis=-1, keepdims=True)
        gain = gain_ref[:, pl.ds(pl.multiple_of(gain_at + (first + i) * DH, DH), DH)]
        o_ref[:, cols] = (raw * lax.rsqrt(square + 1e-06) * gain).astype(o_ref.dtype)
        return carry

    lax.fori_loop(0, count, one, 0, unroll=UNROLL)


def layer_kernel(
    cq, ck, cv, rq, rk, rv, lengths, gain_ref,
    cat_out, resp_out,
    x_ref, got, payload, total_ref, before, totals, partner_totals, cat_inner, resp_inner,
    sends, recvs,
):
    peers, half = x_ref.shape[0], x_ref.shape[1]
    heads_here = cq.shape[1] // DH
    me = lax.axis_index("seq")
    side = lax.axis_index("resp")
    mesh_ids = pl.DeviceIdType.MESH
    barrier = pltpu.get_barrier_semaphore()

    def greet(t, carry):
        pl.semaphore_signal(
            barrier, 1, device_id={"seq": lax.rem(me + t, peers)}, device_id_type=mesh_ids
        )
        return carry

    lax.fori_loop(1, peers, greet, 0)
    pl.semaphore_signal(barrier, 1, device_id={"resp": 1 - side}, device_id_type=mesh_ids)

    def own_state(h, carry):
        cols = pl.ds(pl.multiple_of(h * DH, DH), DH)
        value = lax.dot_general(
            ck[:, cols], cv[:, cols], (((0,), (0,)), ((), ())),
            preferred_element_type=jnp.float32,
        )
        put_head_state(x_ref, h, value, half)
        return carry

    lax.fori_loop(0, heads_here, own_state, 0, unroll=UNROLL)
    pl.semaphore_wait(barrier, peers)

    part = half // PARTS

    def start_all(phase, src_of, dst, k):
        def start(t, carry):
            peer = lax.rem(me + t, peers)
            pltpu.make_async_remote_copy(
                src_ref=src_of(peer),
                dst_ref=dst.at[me, pl.ds(k * part, part)],
                send_sem=sends.at[phase],
                recv_sem=recvs.at[phase],
                device_id={"seq": peer},
                device_id_type=mesh_ids,
            ).start()
            return carry

        lax.fori_loop(1, peers, start, 0)

    def wait_all(phase, dst, k):
        others = pl.ds(0, peers - 1)
        everyone = pltpu.make_async_remote_copy(
            src_ref=dst.at[others, pl.ds(k * part, part)],
            dst_ref=dst.at[others, pl.ds(k * part, part)],
            send_sem=sends.at[phase],
            recv_sem=recvs.at[phase],
            device_id={"seq": lax.rem(me + 1, peers)},
            device_id_type=mesh_ids,
        )
        everyone.wait_send()
        everyone.wait_recv()

    for k in range(PARTS):
        start_all(k, lambda peer, k=k: x_ref.at[peer, pl.ds(k * part, part)], got, k)
    got[pl.ds(me, 1)] = x_ref[pl.ds(me, 1)]
    rows = lax.broadcasted_iota(jnp.int32, (cq.shape[0], cq.shape[0]), 0)
    cols = lax.broadcasted_iota(jnp.int32, (cq.shape[0], cq.shape[0]), 1)
    heads_inner(cq, ck, cv, cols <= rows, cat_inner)

    for k in range(PARTS):
        wait_all(k, got, k)
        rows_k = pl.ds(k * part, part)

        def running(j, acc, rows_k=rows_k):
            payload[pl.ds(j, 1), rows_k] = acc[None]
            return acc + got[j, rows_k]

        total_ref[:, rows_k] = lax.fori_loop(
            0, peers, running, jnp.zeros((part, DH), jnp.float32), unroll=8
        )[None]
        start_all(PARTS + k, lambda peer, rows_k=rows_k: payload.at[peer, rows_k], before, k)
        start_all(2 * PARTS + k, lambda peer, rows_k=rows_k: total_ref.at[0, rows_k], totals, k)
    before[pl.ds(me, 1)] = payload[pl.ds(me, 1)]
    totals[pl.ds(me, 1)] = total_ref[...]
    rrows = lax.broadcasted_iota(jnp.int32, (rq.shape[0], rq.shape[0]), 0)
    rcols = lax.broadcasted_iota(jnp.int32, (rq.shape[0], rq.shape[0]), 1)
    end = lengths[0, 0]
    row_seg = (rrows >= end).astype(jnp.int32)
    col_seg = (rcols >= end).astype(jnp.int32)
    for k in range(1, lengths.shape[1]):
        end = end + lengths[0, k]
        row_seg = row_seg + (rrows >= end).astype(jnp.int32)
        col_seg = col_seg + (rcols >= end).astype(jnp.int32)
    heads_inner(rq, rk, rv, (row_seg == col_seg) & (rcols <= rrows), resp_inner)

    for k in range(PARTS):
        wait_all(PARTS + k, before, k)
    heads_finish(
        cq, cat_inner, lambda i: head_state(before, i, 0, half), gain_ref,
        side * cq.shape[1], 0, heads_here, cat_out,
    )
    for k in range(PARTS):
        wait_all(2 * PARTS + k, totals, k)
    partner = pltpu.make_async_remote_copy(
        src_ref=totals,
        dst_ref=partner_totals,
        send_sem=sends.at[3 * PARTS],
        recv_sem=recvs.at[3 * PARTS],
        device_id={"resp": 1 - side},
        device_id_type=mesh_ids,
    )
    partner.start()
    heads_finish(
        rq, resp_inner, lambda i: head_state(totals, i, 0, half), gain_ref,
        0, side * heads_here, heads_here, resp_out,
    )
    partner.wait_send()
    partner.wait_recv()
    heads_finish(
        rq, resp_inner, lambda i: head_state(partner_totals, i, 0, half), gain_ref,
        0, (1 - side) * heads_here, heads_here, resp_out,
    )


def layer(cat, resp, lengths, gain):
    peers = lax.axis_size("seq")
    half = cat[0].shape[1] // peers
    vmem = pl.BlockSpec(memory_space=pltpu.VMEM)
    cat_rows, cat_width = cat[0].shape
    resp_rows, resp_width = resp[0].shape
    return pl.pallas_call(
        layer_kernel,
        out_shape=(
            jax.ShapeDtypeStruct(cat[0].shape, jnp.bfloat16),
            jax.ShapeDtypeStruct(resp[0].shape, jnp.bfloat16),
        ),
        in_specs=[vmem] * 6 + [pl.BlockSpec(memory_space=pltpu.SMEM), vmem],
        out_specs=(vmem, vmem),
        scratch_shapes=[
            pltpu.VMEM((peers, half, DH), jnp.float32),
            pltpu.VMEM((peers, half, DH), jnp.float32),
            pltpu.VMEM((peers, half, DH), jnp.float32),
            pltpu.VMEM((1, half, DH), jnp.float32),
            pltpu.VMEM((peers, half, DH), jnp.float32),
            pltpu.VMEM((peers, half, DH), jnp.float32),
            pltpu.VMEM((peers, half, DH), jnp.float32),
            pltpu.VMEM(cat[0].shape, jnp.float32),
            pltpu.VMEM(resp[0].shape, jnp.float32),
            pltpu.SemaphoreType.DMA((3 * PARTS + 1,)),
            pltpu.SemaphoreType.DMA((3 * PARTS + 1,)),
        ],
        compiler_params=pltpu.CompilerParams(collective_id=0, has_side_effects=True),
        cost_estimate=pl.CostEstimate(
            flops=10 * DH * (cat_rows * cat_width + resp_rows * resp_width),
            transcendentals=cat_rows * cat_width // DH + resp_rows * resp_width // DH,
            bytes_accessed=14 * peers * half * DH,
        ),
    )(*cat, *resp, lengths, gain)


def per_device(
    cat_query, cat_key, cat_value, resp_query, resp_key, resp_value, resp_lengths, norm_gain
):
    return layer(
        (cat_query, cat_key, cat_value),
        (resp_query, resp_key, resp_value),
        resp_lengths,
        norm_gain.reshape(1, -1),
    )


def solution(mesh):
    placed = (
        P("seq", "resp"),
        P("seq", "resp"),
        P("seq", "resp"),
        P(("seq", "resp"), None),
        P(("seq", "resp"), None),
        P(("seq", "resp"), None),
        P(("seq", "resp"), None),
        P(),
    )
    return jax.shard_map(
        per_device,
        mesh=mesh,
        in_specs=placed,
        out_specs=(P("seq", "resp"), P(("seq", "resp"), None)),
        check_vma=False,
    )
```

```python
import jax
import jax.numpy as jnp
from jax import lax
from jax.experimental import pallas as pl
from jax.experimental.pallas import tpu as pltpu
from jax.sharding import PartitionSpec as P

DH = 128
UNROLL = 8


def block_state(key, value, heads):
    rows = key.shape[0]
    kh = key.reshape(rows, heads, DH)
    vh = value.reshape(rows, heads, DH)
    return jnp.einsum("shd,she->hde", kh, vh, preferred_element_type=jnp.float32)


def heads_inner(q_ref, k_ref, v_ref, keep, o_ref):
    def one(h, carry):
        cols = pl.ds(pl.multiple_of(h * DH, DH), DH)
        scores = lax.dot_general(
            q_ref[:, cols], k_ref[:, cols], (((1,), (1,)), ((), ())),
            preferred_element_type=jnp.float32,
        )
        scores = jnp.where(keep, scores, 0.0).astype(jnp.bfloat16)
        o_ref[:, cols] = jnp.dot(scores, v_ref[:, cols], preferred_element_type=jnp.float32)
        return carry

    lax.fori_loop(0, q_ref.shape[1] // DH, one, 0, unroll=UNROLL)


def split_dot(q, state):
    hi = state.astype(jnp.bfloat16)
    rest = state - hi.astype(jnp.float32)
    mid = rest.astype(jnp.bfloat16)
    lo = (rest - mid.astype(jnp.float32)).astype(jnp.bfloat16)
    acc = jnp.dot(q, hi, preferred_element_type=jnp.float32)
    acc = acc + jnp.dot(q, mid, preferred_element_type=jnp.float32)
    return acc + jnp.dot(q, lo, preferred_element_type=jnp.float32)


def head_state(ref, h, first, half):
    if half <= DH:
        group = DH // half
        return ref[pl.ds(h * group, group), pl.ds(first, half), :].reshape(DH, DH)
    per = half // DH
    return ref[h // per, pl.ds(first + (h % per) * DH, DH), :]


def put_head_state(ref, h, value, half):
    if half <= DH:
        group = DH // half
        ref[pl.ds(h * group, group)] = value.reshape(group, half, DH)
    else:
        per = half // DH
        ref[h // per, pl.ds((h % per) * DH, DH), :] = value


def heads_finish(q_ref, inner_ref, state_of, gain_ref, gain_at, first, count, o_ref):
    def one(i, carry):
        cols = pl.ds(pl.multiple_of((first + i) * DH, DH), DH)
        raw = inner_ref[:, cols] + split_dot(q_ref[:, cols], state_of(i))
        square = jnp.mean(raw * raw, axis=-1, keepdims=True)
        gain = gain_ref[:, pl.ds(pl.multiple_of(gain_at + (first + i) * DH, DH), DH)]
        o_ref[:, cols] = (raw * lax.rsqrt(square + 1e-06) * gain).astype(o_ref.dtype)
        return carry

    lax.fori_loop(0, count, one, 0, unroll=UNROLL)


def layer_kernel(
    cq, ck, cv, rq, rk, rv, lengths, gain_ref,
    cat_out, resp_out,
    x_ref, got, payload, total_ref, before, totals, partner_totals, cat_inner, resp_inner,
    sends, recvs,
):
    peers, half = x_ref.shape[0], x_ref.shape[1]
    heads_here = cq.shape[1] // DH
    me = lax.axis_index("seq")
    side = lax.axis_index("resp")
    mesh_ids = pl.DeviceIdType.MESH
    barrier = pltpu.get_barrier_semaphore()

    def greet(t, carry):
        pl.semaphore_signal(
            barrier, 1, device_id={"seq": lax.rem(me + t, peers)}, device_id_type=mesh_ids
        )
        return carry

    lax.fori_loop(1, peers, greet, 0)
    pl.semaphore_signal(barrier, 1, device_id={"resp": 1 - side}, device_id_type=mesh_ids)

    def own_state(h, carry):
        cols = pl.ds(pl.multiple_of(h * DH, DH), DH)
        value = lax.dot_general(
            ck[:, cols], cv[:, cols], (((0,), (0,)), ((), ())),
            preferred_element_type=jnp.float32,
        )
        put_head_state(x_ref, h, value, half)
        return carry

    lax.fori_loop(0, heads_here, own_state, 0, unroll=UNROLL)
    pl.semaphore_wait(barrier, peers)

    part = half // 2

    def start_all(phase, src_of, dst, k):
        def start(t, carry):
            peer = lax.rem(me + t, peers)
            pltpu.make_async_remote_copy(
                src_ref=src_of(peer),
                dst_ref=dst.at[me, pl.ds(k * part, part)],
                send_sem=sends.at[phase],
                recv_sem=recvs.at[phase],
                device_id={"seq": peer},
                device_id_type=mesh_ids,
            ).start()
            return carry

        lax.fori_loop(1, peers, start, 0)

    def wait_all(phase, dst, k):
        others = pl.ds(0, peers - 1)
        everyone = pltpu.make_async_remote_copy(
            src_ref=dst.at[others, pl.ds(k * part, part)],
            dst_ref=dst.at[others, pl.ds(k * part, part)],
            send_sem=sends.at[phase],
            recv_sem=recvs.at[phase],
            device_id={"seq": lax.rem(me + 1, peers)},
            device_id_type=mesh_ids,
        )
        everyone.wait_send()
        everyone.wait_recv()

    for k in range(2):
        start_all(k, lambda peer, k=k: x_ref.at[peer, pl.ds(k * part, part)], got, k)
    got[pl.ds(me, 1)] = x_ref[pl.ds(me, 1)]
    rows = lax.broadcasted_iota(jnp.int32, (cq.shape[0], cq.shape[0]), 0)
    cols = lax.broadcasted_iota(jnp.int32, (cq.shape[0], cq.shape[0]), 1)
    heads_inner(cq, ck, cv, cols <= rows, cat_inner)

    for k in range(2):
        wait_all(k, got, k)
        rows_k = pl.ds(k * part, part)

        def running(j, acc, rows_k=rows_k):
            payload[pl.ds(j, 1), rows_k] = acc[None]
            return acc + got[j, rows_k]

        total_ref[:, rows_k] = lax.fori_loop(
            0, peers, running, jnp.zeros((part, DH), jnp.float32), unroll=8
        )[None]
        start_all(4 + k, lambda peer, rows_k=rows_k: total_ref.at[0, rows_k], totals, k)
        start_all(2 + k, lambda peer, rows_k=rows_k: payload.at[peer, rows_k], before, k)
    before[pl.ds(me, 1)] = payload[pl.ds(me, 1)]
    totals[pl.ds(me, 1)] = total_ref[...]
    rrows = lax.broadcasted_iota(jnp.int32, (rq.shape[0], rq.shape[0]), 0)
    rcols = lax.broadcasted_iota(jnp.int32, (rq.shape[0], rq.shape[0]), 1)
    end = lengths[0, 0]
    row_seg = (rrows >= end).astype(jnp.int32)
    col_seg = (rcols >= end).astype(jnp.int32)
    for k in range(1, lengths.shape[1]):
        end = end + lengths[0, k]
        row_seg = row_seg + (rrows >= end).astype(jnp.int32)
        col_seg = col_seg + (rcols >= end).astype(jnp.int32)
    heads_inner(rq, rk, rv, (row_seg == col_seg) & (rcols <= rrows), resp_inner)

    wait_all(4, totals, 0)
    wait_all(5, totals, 1)
    partner = pltpu.make_async_remote_copy(
        src_ref=totals,
        dst_ref=partner_totals,
        send_sem=sends.at[6],
        recv_sem=recvs.at[6],
        device_id={"resp": 1 - side},
        device_id_type=mesh_ids,
    )
    partner.start()
    heads_finish(
        rq, resp_inner, lambda i: head_state(totals, i, 0, half), gain_ref,
        0, side * heads_here, heads_here, resp_out,
    )
    partner.wait_send()
    partner.wait_recv()
    heads_finish(
        rq, resp_inner, lambda i: head_state(partner_totals, i, 0, half), gain_ref,
        0, (1 - side) * heads_here, heads_here, resp_out,
    )
    wait_all(2, before, 0)
    wait_all(3, before, 1)
    heads_finish(
        cq, cat_inner, lambda i: head_state(before, i, 0, half), gain_ref,
        side * cq.shape[1], 0, heads_here, cat_out,
    )


def layer(cat, resp, lengths, gain):
    peers = lax.axis_size("seq")
    half = cat[0].shape[1] // peers
    vmem = pl.BlockSpec(memory_space=pltpu.VMEM)
    cat_rows, cat_width = cat[0].shape
    resp_rows, resp_width = resp[0].shape
    return pl.pallas_call(
        layer_kernel,
        out_shape=(
            jax.ShapeDtypeStruct(cat[0].shape, jnp.bfloat16),
            jax.ShapeDtypeStruct(resp[0].shape, jnp.bfloat16),
        ),
        in_specs=[vmem] * 6 + [pl.BlockSpec(memory_space=pltpu.SMEM), vmem],
        out_specs=(vmem, vmem),
        scratch_shapes=[
            pltpu.VMEM((peers, half, DH), jnp.float32),
            pltpu.VMEM((peers, half, DH), jnp.float32),
            pltpu.VMEM((peers, half, DH), jnp.float32),
            pltpu.VMEM((1, half, DH), jnp.float32),
            pltpu.VMEM((peers, half, DH), jnp.float32),
            pltpu.VMEM((peers, half, DH), jnp.float32),
            pltpu.VMEM((peers, half, DH), jnp.float32),
            pltpu.VMEM(cat[0].shape, jnp.float32),
            pltpu.VMEM(resp[0].shape, jnp.float32),
            pltpu.SemaphoreType.DMA((7,)),
            pltpu.SemaphoreType.DMA((7,)),
        ],
        compiler_params=pltpu.CompilerParams(collective_id=0, has_side_effects=True),
        cost_estimate=pl.CostEstimate(
            flops=10 * DH * (cat_rows * cat_width + resp_rows * resp_width),
            transcendentals=cat_rows * cat_width // DH + resp_rows * resp_width // DH,
            bytes_accessed=14 * peers * half * DH,
        ),
    )(*cat, *resp, lengths, gain)


def per_device(
    cat_query, cat_key, cat_value, resp_query, resp_key, resp_value, resp_lengths, norm_gain
):
    return layer(
        (cat_query, cat_key, cat_value),
        (resp_query, resp_key, resp_value),
        resp_lengths,
        norm_gain.reshape(1, -1),
    )


def solution(mesh):
    placed = (
        P("seq", "resp"),
        P("seq", "resp"),
        P("seq", "resp"),
        P(("seq", "resp"), None),
        P(("seq", "resp"), None),
        P(("seq", "resp"), None),
        P(("seq", "resp"), None),
        P(),
    )
    return jax.shard_map(
        per_device,
        mesh=mesh,
        in_specs=placed,
        out_specs=(P("seq", "resp"), P(("seq", "resp"), None)),
        check_vma=False,
    )
```

```python
import jax
import jax.numpy as jnp
from jax import lax
from jax.experimental import pallas as pl
from jax.experimental.pallas import tpu as pltpu
from jax.sharding import PartitionSpec as P

DH = 128
UNROLL = 8


def block_state(key, value, heads):
    rows = key.shape[0]
    kh = key.reshape(rows, heads, DH)
    vh = value.reshape(rows, heads, DH)
    return jnp.einsum("shd,she->hde", kh, vh, preferred_element_type=jnp.float32)


def heads_inner(q_ref, k_ref, v_ref, keep, o_ref):
    def one(h, carry):
        cols = pl.ds(pl.multiple_of(h * DH, DH), DH)
        scores = lax.dot_general(
            q_ref[:, cols], k_ref[:, cols], (((1,), (1,)), ((), ())),
            preferred_element_type=jnp.float32,
        )
        scores = jnp.where(keep, scores, 0.0).astype(jnp.bfloat16)
        o_ref[:, cols] = jnp.dot(scores, v_ref[:, cols], preferred_element_type=jnp.float32)
        return carry

    lax.fori_loop(0, q_ref.shape[1] // DH, one, 0, unroll=UNROLL)


def split_dot(q, state):
    hi = state.astype(jnp.bfloat16)
    rest = state - hi.astype(jnp.float32)
    mid = rest.astype(jnp.bfloat16)
    lo = (rest - mid.astype(jnp.float32)).astype(jnp.bfloat16)
    acc = jnp.dot(q, hi, preferred_element_type=jnp.float32)
    acc = acc + jnp.dot(q, mid, preferred_element_type=jnp.float32)
    return acc + jnp.dot(q, lo, preferred_element_type=jnp.float32)


def head_state(ref, h, first, half):
    if half <= DH:
        group = DH // half
        return ref[pl.ds(h * group, group), pl.ds(first, half), :].reshape(DH, DH)
    per = half // DH
    return ref[h // per, pl.ds(first + (h % per) * DH, DH), :]


def put_head_state(ref, h, value, half):
    if half <= DH:
        group = DH // half
        ref[pl.ds(h * group, group)] = value.reshape(group, half, DH)
    else:
        per = half // DH
        ref[h // per, pl.ds((h % per) * DH, DH), :] = value


def heads_finish(q_ref, inner_ref, state_of, gain_ref, gain_at, first, count, o_ref):
    def one(i, carry):
        cols = pl.ds(pl.multiple_of((first + i) * DH, DH), DH)
        raw = inner_ref[:, cols] + split_dot(q_ref[:, cols], state_of(i))
        square = jnp.mean(raw * raw, axis=-1, keepdims=True)
        gain = gain_ref[:, pl.ds(pl.multiple_of(gain_at + (first + i) * DH, DH), DH)]
        o_ref[:, cols] = (raw * lax.rsqrt(square + 1e-06) * gain).astype(o_ref.dtype)
        return carry

    lax.fori_loop(0, count, one, 0, unroll=UNROLL)


def layer_kernel(
    cq, ck, cv, rq, rk, rv, lengths, gain_ref,
    cat_out, resp_out,
    x_ref, got, payload, total_ref, before, totals, partner_totals, cat_inner, resp_inner,
    sends, recvs,
):
    peers, half = x_ref.shape[0], x_ref.shape[1]
    heads_here = cq.shape[1] // DH
    me = lax.axis_index("seq")
    side = lax.axis_index("resp")
    mesh_ids = pl.DeviceIdType.MESH
    barrier = pltpu.get_barrier_semaphore()

    def greet(t, carry):
        pl.semaphore_signal(
            barrier, 1, device_id={"seq": lax.rem(me + t, peers)}, device_id_type=mesh_ids
        )
        return carry

    lax.fori_loop(1, peers, greet, 0)
    pl.semaphore_signal(barrier, 1, device_id={"resp": 1 - side}, device_id_type=mesh_ids)

    def own_state(h, carry):
        cols = pl.ds(pl.multiple_of(h * DH, DH), DH)
        value = lax.dot_general(
            ck[:, cols], cv[:, cols], (((0,), (0,)), ((), ())),
            preferred_element_type=jnp.float32,
        )
        put_head_state(x_ref, h, value, half)
        return carry

    lax.fori_loop(0, heads_here, own_state, 0, unroll=UNROLL)
    pl.semaphore_wait(barrier, peers)

    part = half // 2

    def start_all(phase, src_of, dst, k):
        def start(t, carry):
            peer = lax.rem(me + t, peers)
            pltpu.make_async_remote_copy(
                src_ref=src_of(peer),
                dst_ref=dst.at[me, pl.ds(k * part, part)],
                send_sem=sends.at[phase],
                recv_sem=recvs.at[phase],
                device_id={"seq": peer},
                device_id_type=mesh_ids,
            ).start()
            return carry

        lax.fori_loop(1, peers, start, 0)

    def wait_all(phase, dst, k):
        others = pl.ds(0, peers - 1)
        everyone = pltpu.make_async_remote_copy(
            src_ref=dst.at[others, pl.ds(k * part, part)],
            dst_ref=dst.at[others, pl.ds(k * part, part)],
            send_sem=sends.at[phase],
            recv_sem=recvs.at[phase],
            device_id={"seq": lax.rem(me + 1, peers)},
            device_id_type=mesh_ids,
        )
        everyone.wait_send()
        everyone.wait_recv()

    for k in range(2):
        start_all(k, lambda peer, k=k: x_ref.at[peer, pl.ds(k * part, part)], got, k)
    got[pl.ds(me, 1)] = x_ref[pl.ds(me, 1)]
    rows = lax.broadcasted_iota(jnp.int32, (cq.shape[0], cq.shape[0]), 0)
    cols = lax.broadcasted_iota(jnp.int32, (cq.shape[0], cq.shape[0]), 1)
    heads_inner(cq, ck, cv, cols <= rows, cat_inner)

    for k in range(2):
        wait_all(k, got, k)
        rows_k = pl.ds(k * part, part)

        def running(j, acc, rows_k=rows_k):
            payload[pl.ds(j, 1), rows_k] = acc[None]
            return acc + got[j, rows_k]

        total_ref[:, rows_k] = lax.fori_loop(
            0, peers, running, jnp.zeros((part, DH), jnp.float32), unroll=8
        )[None]
        start_all(4 + k, lambda peer, rows_k=rows_k: total_ref.at[0, rows_k], totals, k)
        start_all(2 + k, lambda peer, rows_k=rows_k: payload.at[peer, rows_k], before, k)
    before[pl.ds(me, 1)] = payload[pl.ds(me, 1)]
    totals[pl.ds(me, 1)] = total_ref[...]
    rrows = lax.broadcasted_iota(jnp.int32, (rq.shape[0], rq.shape[0]), 0)
    rcols = lax.broadcasted_iota(jnp.int32, (rq.shape[0], rq.shape[0]), 1)
    end = lengths[0, 0]
    row_seg = (rrows >= end).astype(jnp.int32)
    col_seg = (rcols >= end).astype(jnp.int32)
    for k in range(1, lengths.shape[1]):
        end = end + lengths[0, k]
        row_seg = row_seg + (rrows >= end).astype(jnp.int32)
        col_seg = col_seg + (rcols >= end).astype(jnp.int32)
    heads_inner(rq, rk, rv, (row_seg == col_seg) & (rcols <= rrows), resp_inner)

    forwards = []
    for k in range(2):
        wait_all(4 + k, totals, k)
        forward = pltpu.make_async_remote_copy(
            src_ref=totals.at[:, pl.ds(k * part, part)],
            dst_ref=partner_totals.at[:, pl.ds(k * part, part)],
            send_sem=sends.at[6 + k],
            recv_sem=recvs.at[6 + k],
            device_id={"resp": 1 - side},
            device_id_type=mesh_ids,
        )
        forward.start()
        forwards.append(forward)
    heads_finish(
        rq, resp_inner, lambda i: head_state(totals, i, 0, half), gain_ref,
        0, side * heads_here, heads_here, resp_out,
    )
    for forward in forwards:
        forward.wait_send()
        forward.wait_recv()
    heads_finish(
        rq, resp_inner, lambda i: head_state(partner_totals, i, 0, half), gain_ref,
        0, (1 - side) * heads_here, heads_here, resp_out,
    )
    wait_all(2, before, 0)
    wait_all(3, before, 1)
    heads_finish(
        cq, cat_inner, lambda i: head_state(before, i, 0, half), gain_ref,
        side * cq.shape[1], 0, heads_here, cat_out,
    )


def layer(cat, resp, lengths, gain):
    peers = lax.axis_size("seq")
    half = cat[0].shape[1] // peers
    vmem = pl.BlockSpec(memory_space=pltpu.VMEM)
    cat_rows, cat_width = cat[0].shape
    resp_rows, resp_width = resp[0].shape
    return pl.pallas_call(
        layer_kernel,
        out_shape=(
            jax.ShapeDtypeStruct(cat[0].shape, jnp.bfloat16),
            jax.ShapeDtypeStruct(resp[0].shape, jnp.bfloat16),
        ),
        in_specs=[vmem] * 6 + [pl.BlockSpec(memory_space=pltpu.SMEM), vmem],
        out_specs=(vmem, vmem),
        scratch_shapes=[
            pltpu.VMEM((peers, half, DH), jnp.float32),
            pltpu.VMEM((peers, half, DH), jnp.float32),
            pltpu.VMEM((peers, half, DH), jnp.float32),
            pltpu.VMEM((1, half, DH), jnp.float32),
            pltpu.VMEM((peers, half, DH), jnp.float32),
            pltpu.VMEM((peers, half, DH), jnp.float32),
            pltpu.VMEM((peers, half, DH), jnp.float32),
            pltpu.VMEM(cat[0].shape, jnp.float32),
            pltpu.VMEM(resp[0].shape, jnp.float32),
            pltpu.SemaphoreType.DMA((8,)),
            pltpu.SemaphoreType.DMA((8,)),
        ],
        compiler_params=pltpu.CompilerParams(collective_id=0, has_side_effects=True),
        cost_estimate=pl.CostEstimate(
            flops=10 * DH * (cat_rows * cat_width + resp_rows * resp_width),
            transcendentals=cat_rows * cat_width // DH + resp_rows * resp_width // DH,
            bytes_accessed=14 * peers * half * DH,
        ),
    )(*cat, *resp, lengths, gain)


def per_device(
    cat_query, cat_key, cat_value, resp_query, resp_key, resp_value, resp_lengths, norm_gain
):
    return layer(
        (cat_query, cat_key, cat_value),
        (resp_query, resp_key, resp_value),
        resp_lengths,
        norm_gain.reshape(1, -1),
    )


def solution(mesh):
    placed = (
        P("seq", "resp"),
        P("seq", "resp"),
        P("seq", "resp"),
        P(("seq", "resp"), None),
        P(("seq", "resp"), None),
        P(("seq", "resp"), None),
        P(("seq", "resp"), None),
        P(),
    )
    return jax.shard_map(
        per_device,
        mesh=mesh,
        in_specs=placed,
        out_specs=(P("seq", "resp"), P(("seq", "resp"), None)),
        check_vma=False,
    )
```

```python
import jax
import jax.numpy as jnp
from jax import lax
from jax.experimental import pallas as pl
from jax.experimental.pallas import tpu as pltpu
from jax.sharding import PartitionSpec as P

DH = 128
UNROLL = 16


def block_state(key, value, heads):
    rows = key.shape[0]
    kh = key.reshape(rows, heads, DH)
    vh = value.reshape(rows, heads, DH)
    return jnp.einsum("shd,she->hde", kh, vh, preferred_element_type=jnp.float32)


def heads_inner(q_ref, k_ref, v_ref, keep, o_ref):
    def one(h, carry):
        cols = pl.ds(pl.multiple_of(h * DH, DH), DH)
        scores = lax.dot_general(
            q_ref[:, cols], k_ref[:, cols], (((1,), (1,)), ((), ())),
            preferred_element_type=jnp.float32,
        )
        scores = jnp.where(keep, scores, 0.0).astype(jnp.bfloat16)
        o_ref[:, cols] = jnp.dot(scores, v_ref[:, cols], preferred_element_type=jnp.float32)
        return carry

    lax.fori_loop(0, q_ref.shape[1] // DH, one, 0, unroll=UNROLL)


def split_dot(q, state):
    hi = state.astype(jnp.bfloat16)
    rest = state - hi.astype(jnp.float32)
    mid = rest.astype(jnp.bfloat16)
    lo = (rest - mid.astype(jnp.float32)).astype(jnp.bfloat16)
    acc = jnp.dot(q, hi, preferred_element_type=jnp.float32)
    acc = acc + jnp.dot(q, mid, preferred_element_type=jnp.float32)
    return acc + jnp.dot(q, lo, preferred_element_type=jnp.float32)


def head_state(ref, h, first, half):
    if half <= DH:
        group = DH // half
        return ref[pl.ds(h * group, group), pl.ds(first, half), :].reshape(DH, DH)
    per = half // DH
    return ref[h // per, pl.ds(first + (h % per) * DH, DH), :]


def put_head_state(ref, h, value, half):
    if half <= DH:
        group = DH // half
        ref[pl.ds(h * group, group)] = value.reshape(group, half, DH)
    else:
        per = half // DH
        ref[h // per, pl.ds((h % per) * DH, DH), :] = value


def heads_finish(q_ref, inner_ref, state_of, gain_ref, gain_at, first, count, o_ref):
    def one(i, carry):
        cols = pl.ds(pl.multiple_of((first + i) * DH, DH), DH)
        raw = inner_ref[:, cols] + split_dot(q_ref[:, cols], state_of(i))
        square = jnp.mean(raw * raw, axis=-1, keepdims=True)
        gain = gain_ref[:, pl.ds(pl.multiple_of(gain_at + (first + i) * DH, DH), DH)]
        o_ref[:, cols] = (raw * lax.rsqrt(square + 1e-06) * gain).astype(o_ref.dtype)
        return carry

    lax.fori_loop(0, count, one, 0, unroll=UNROLL)


def layer_kernel(
    cq, ck, cv, rq, rk, rv, lengths, gain_ref,
    cat_out, resp_out,
    x_ref, got, payload, total_ref, before, totals, partner_totals, cat_inner, resp_inner,
    sends, recvs,
):
    peers, half = x_ref.shape[0], x_ref.shape[1]
    heads_here = cq.shape[1] // DH
    me = lax.axis_index("seq")
    side = lax.axis_index("resp")
    mesh_ids = pl.DeviceIdType.MESH
    barrier = pltpu.get_barrier_semaphore()

    def greet(t, carry):
        pl.semaphore_signal(
            barrier, 1, device_id={"seq": lax.rem(me + t, peers)}, device_id_type=mesh_ids
        )
        return carry

    lax.fori_loop(1, peers, greet, 0)
    pl.semaphore_signal(barrier, 1, device_id={"resp": 1 - side}, device_id_type=mesh_ids)

    def own_state(h, carry):
        cols = pl.ds(pl.multiple_of(h * DH, DH), DH)
        value = lax.dot_general(
            ck[:, cols], cv[:, cols], (((0,), (0,)), ((), ())),
            preferred_element_type=jnp.float32,
        )
        put_head_state(x_ref, h, value, half)
        return carry

    lax.fori_loop(0, heads_here, own_state, 0, unroll=UNROLL)
    pl.semaphore_wait(barrier, peers)

    part = half // 2

    def start_all(phase, src_of, dst, k):
        def start(t, carry):
            peer = lax.rem(me + t, peers)
            pltpu.make_async_remote_copy(
                src_ref=src_of(peer),
                dst_ref=dst.at[me, pl.ds(k * part, part)],
                send_sem=sends.at[phase],
                recv_sem=recvs.at[phase],
                device_id={"seq": peer},
                device_id_type=mesh_ids,
            ).start()
            return carry

        lax.fori_loop(1, peers, start, 0)

    def wait_all(phase, dst, k):
        others = pl.ds(0, peers - 1)
        everyone = pltpu.make_async_remote_copy(
            src_ref=dst.at[others, pl.ds(k * part, part)],
            dst_ref=dst.at[others, pl.ds(k * part, part)],
            send_sem=sends.at[phase],
            recv_sem=recvs.at[phase],
            device_id={"seq": lax.rem(me + 1, peers)},
            device_id_type=mesh_ids,
        )
        everyone.wait_send()
        everyone.wait_recv()

    for k in range(2):
        start_all(k, lambda peer, k=k: x_ref.at[peer, pl.ds(k * part, part)], got, k)
    got[pl.ds(me, 1)] = x_ref[pl.ds(me, 1)]
    rows = lax.broadcasted_iota(jnp.int32, (cq.shape[0], cq.shape[0]), 0)
    cols = lax.broadcasted_iota(jnp.int32, (cq.shape[0], cq.shape[0]), 1)
    heads_inner(cq, ck, cv, cols <= rows, cat_inner)

    for k in range(2):
        wait_all(k, got, k)
        rows_k = pl.ds(k * part, part)

        def running(j, acc, rows_k=rows_k):
            payload[pl.ds(j, 1), rows_k] = acc[None]
            return acc + got[j, rows_k]

        total_ref[:, rows_k] = lax.fori_loop(
            0, peers, running, jnp.zeros((part, DH), jnp.float32), unroll=8
        )[None]
        start_all(4 + k, lambda peer, rows_k=rows_k: total_ref.at[0, rows_k], totals, k)
        start_all(2 + k, lambda peer, rows_k=rows_k: payload.at[peer, rows_k], before, k)
    before[pl.ds(me, 1)] = payload[pl.ds(me, 1)]
    totals[pl.ds(me, 1)] = total_ref[...]
    rrows = lax.broadcasted_iota(jnp.int32, (rq.shape[0], rq.shape[0]), 0)
    rcols = lax.broadcasted_iota(jnp.int32, (rq.shape[0], rq.shape[0]), 1)
    end = lengths[0, 0]
    row_seg = (rrows >= end).astype(jnp.int32)
    col_seg = (rcols >= end).astype(jnp.int32)
    for k in range(1, lengths.shape[1]):
        end = end + lengths[0, k]
        row_seg = row_seg + (rrows >= end).astype(jnp.int32)
        col_seg = col_seg + (rcols >= end).astype(jnp.int32)
    heads_inner(rq, rk, rv, (row_seg == col_seg) & (rcols <= rrows), resp_inner)

    wait_all(4, totals, 0)
    wait_all(5, totals, 1)
    partner = pltpu.make_async_remote_copy(
        src_ref=totals,
        dst_ref=partner_totals,
        send_sem=sends.at[6],
        recv_sem=recvs.at[6],
        device_id={"resp": 1 - side},
        device_id_type=mesh_ids,
    )
    partner.start()
    heads_finish(
        rq, resp_inner, lambda i: head_state(totals, i, 0, half), gain_ref,
        0, side * heads_here, heads_here, resp_out,
    )
    partner.wait_send()
    partner.wait_recv()
    heads_finish(
        rq, resp_inner, lambda i: head_state(partner_totals, i, 0, half), gain_ref,
        0, (1 - side) * heads_here, heads_here, resp_out,
    )
    wait_all(2, before, 0)
    wait_all(3, before, 1)
    heads_finish(
        cq, cat_inner, lambda i: head_state(before, i, 0, half), gain_ref,
        side * cq.shape[1], 0, heads_here, cat_out,
    )


def layer(cat, resp, lengths, gain):
    peers = lax.axis_size("seq")
    half = cat[0].shape[1] // peers
    vmem = pl.BlockSpec(memory_space=pltpu.VMEM)
    cat_rows, cat_width = cat[0].shape
    resp_rows, resp_width = resp[0].shape
    return pl.pallas_call(
        layer_kernel,
        out_shape=(
            jax.ShapeDtypeStruct(cat[0].shape, jnp.bfloat16),
            jax.ShapeDtypeStruct(resp[0].shape, jnp.bfloat16),
        ),
        in_specs=[vmem] * 6 + [pl.BlockSpec(memory_space=pltpu.SMEM), vmem],
        out_specs=(vmem, vmem),
        scratch_shapes=[
            pltpu.VMEM((peers, half, DH), jnp.float32),
            pltpu.VMEM((peers, half, DH), jnp.float32),
            pltpu.VMEM((peers, half, DH), jnp.float32),
            pltpu.VMEM((1, half, DH), jnp.float32),
            pltpu.VMEM((peers, half, DH), jnp.float32),
            pltpu.VMEM((peers, half, DH), jnp.float32),
            pltpu.VMEM((peers, half, DH), jnp.float32),
            pltpu.VMEM(cat[0].shape, jnp.float32),
            pltpu.VMEM(resp[0].shape, jnp.float32),
            pltpu.SemaphoreType.DMA((7,)),
            pltpu.SemaphoreType.DMA((7,)),
        ],
        compiler_params=pltpu.CompilerParams(collective_id=0, has_side_effects=True),
        cost_estimate=pl.CostEstimate(
            flops=10 * DH * (cat_rows * cat_width + resp_rows * resp_width),
            transcendentals=cat_rows * cat_width // DH + resp_rows * resp_width // DH,
            bytes_accessed=14 * peers * half * DH,
        ),
    )(*cat, *resp, lengths, gain)


def per_device(
    cat_query, cat_key, cat_value, resp_query, resp_key, resp_value, resp_lengths, norm_gain
):
    return layer(
        (cat_query, cat_key, cat_value),
        (resp_query, resp_key, resp_value),
        resp_lengths,
        norm_gain.reshape(1, -1),
    )


def solution(mesh):
    placed = (
        P("seq", "resp"),
        P("seq", "resp"),
        P("seq", "resp"),
        P(("seq", "resp"), None),
        P(("seq", "resp"), None),
        P(("seq", "resp"), None),
        P(("seq", "resp"), None),
        P(),
    )
    return jax.shard_map(
        per_device,
        mesh=mesh,
        in_specs=placed,
        out_specs=(P("seq", "resp"), P(("seq", "resp"), None)),
        check_vma=False,
    )
```
